128 devices in a mesh: view: 32 (over z, y, core), plane: 4 (over x).
Axes of the slice: x: 4, y: 4, z: 4, core: 2. Of those that a mesh axis runs over, the one named last changes fastest.
Arguments:
- features: bfloat16 [128, 32, 512], P('view'), may hold values from -6 to 6
- sources: int32 [128, 10], replicated, may hold values from 0 to 127, as said below
- warp_weights: bfloat16 [48, 512, 512], P('plane'), may hold values from -0.25 to 0.25
- view_gate: float32 [8], replicated, may hold values from -6 to 6
- depth_kernel: float32 [3, 8, 8], replicated, may hold values from -4 to 4
- cotangent: bfloat16 [128, 48, 8, 512], P('view', 'plane'), may hold values from -6 to 6
Outputs:
- regular: bfloat16 [128, 48, 8, 512], P('view', 'plane')
- feature_grads: float32 [128, 32, 512], P('view')
The draws below stay inside these ranges and needn't reach their ends.
Inputs may be any that keep to these rules, and one draw needn't show every extreme that they name: `sources`: view v is owned by the device at index v // 4 of view. Among the 40 entries of the rows of one device (rows i * 4 to i * 4 + 3), at most 3 name views of any one owner, and for each device some owner is named exactly 3 times.
All inputs are finite; a program needn't handle non-finite values.
Results may differ from the reference program's by a relative error of at most 0.0038.
Values may be sent and summed in bfloat16 or wider, within the bound.
A program may use at most 128 MiB of HBM per device.

```python
import jax
import jax.numpy as jnp
from jax import lax

C = 32
G = 8
GC = 4
D = 48
S = 10
VIEWS_DEV = 4
PIX = 512
NV = 128
CAP = 3


def draw_sources(key, part):
    blocks = NV // VIEWS_DEV
    requests = VIEWS_DEV * S
    slot_total = blocks * CAP

    def one_block(block_key):
        first, second, third, fourth = jax.random.split(block_key, 4)
        busiest = jax.random.randint(first, (), 0, blocks)
        order = jax.random.permutation(second, slot_total)
        owners = order // CAP
        sort_key = jnp.where(owners == busiest, 0, slot_total) + jnp.arange(slot_total)
        chosen = owners[jnp.argsort(sort_key)][:requests]
        chosen = chosen[jax.random.permutation(third, requests)]
        local_pick = jax.random.randint(fourth, (requests,), 0, VIEWS_DEV)
        return (chosen * VIEWS_DEV + local_pick).reshape(VIEWS_DEV, S)
    block_keys = jax.random.split(jax.random.fold_in(key, 17), blocks)
    return jax.vmap(one_block)(block_keys).reshape(NV, S).astype(jnp.int32)


def level_of(stream_key, shape, cuts, least, top_value):
    def one(axis_at, blocks):
        steps = jax.random.uniform(jax.random.fold_in(jax.random.fold_in(stream_key, 6), axis_at), (blocks,), jnp.float32, least / len(cuts), top_value / len(cuts))
        return jnp.repeat(jnp.exp(steps), shape[axis_at] // blocks).reshape((-1,) + (1,) * (len(shape) - axis_at - 1))

    factor_of = one(*cuts[0])
    for cut in cuts[1:]:
        factor_of = factor_of * one(*cut)
    return factor_of


def centred(own_key, dims, deviation, bound, shards=(), kind=jnp.bfloat16):
    entries = jax.random.normal(own_key, dims, jnp.float32) * deviation
    if len(shards) > 0:
        entries = level_of(own_key, dims, shards, -0.22, 0.18) * entries
    return jnp.clip(entries, min=-bound, max=bound).astype(kind)


def setup_inputs(seed: int = 0) -> dict:
    splits = jax.random.split(jax.random.key(seed), 7)
    return {
        "features": centred(splits[0], (NV, C, PIX), 1.0, 6.0, ((0, 32),)),
        "sources": draw_sources(jax.random.fold_in(splits[6], 71), 0),
        "warp_weights": centred(splits[2], (D, PIX, PIX), PIX ** -0.5, 0.25, ((0, 4),)),
        "view_gate": centred(splits[3], (G,), 2.0, 6.0, (), jnp.float32),
        "depth_kernel": centred(splits[4], (3, G, G), 1.0, 4.0, (), jnp.float32),
        "cotangent": centred(splits[5], (NV, D, G, PIX), 1.0, 6.0, ((0, 32), (1, 4))),
    }


def aggregate(ref_map, warped, view_gate):
    src_count = warped.shape[0]
    plane_count = warped.shape[1]
    product = ref_map[None, None] * warped
    correlation = lax.optimization_barrier(jnp.sum(product.reshape(src_count, plane_count, G, GC, product.shape[-1]), axis=3)) / GC
    logits = lax.optimization_barrier(jnp.sum(correlation * view_gate[None, None, :, None], axis=2))
    visible = 0.5 + jax.nn.sigmoid(logits)
    weighted = lax.optimization_barrier(jnp.sum(visible[:, :, None, :] * correlation, axis=0))
    return weighted / lax.optimization_barrier(jnp.sum(visible, axis=0))[:, None, :]

def warp_planes(src_maps, warp_weights):
    return jnp.einsum('scy,dxy->sdcx', src_maps.astype(jnp.float32), warp_weights.astype(jnp.float32), precision=lax.Precision.HIGHEST)

def depth_conv(cost_volume, depth_kernel):
    planes = cost_volume.shape[1]
    padded = jnp.pad(cost_volume, ((0, 0), (1, 1), (0, 0), (0, 0)))
    result = jnp.zeros(cost_volume.shape, jnp.float32)
    for offset in range(3):
        result = result + jnp.einsum('og,rdgx->rdox', depth_kernel[offset], padded[:, offset:offset + planes], precision=lax.Precision.HIGHEST)
    return result

def reference(features, sources, warp_weights, view_gate, depth_kernel, cotangent):

    def forward_one(index):
        ref_map = features[index].astype(jnp.float32)
        src_maps = features[sources[index]]
        return aggregate(ref_map, warp_planes(src_maps, warp_weights), view_gate)
    cost_volume = lax.map(forward_one, jnp.arange(NV))
    pre_act, conv_vjp = jax.vjp(lambda volume: depth_conv(volume, depth_kernel), cost_volume)
    regular = jax.nn.silu(pre_act).astype(jnp.bfloat16)
    sigmoid_pre = jax.nn.sigmoid(pre_act)
    pre_grad = cotangent.astype(jnp.float32) * (sigmoid_pre * (1.0 + pre_act * (1.0 - sigmoid_pre)))
    cost_grad = conv_vjp(pre_grad)[0]

    def backward_one(index):
        ref_map = features[index].astype(jnp.float32)
        src_maps = features[sources[index]]
        warped = warp_planes(src_maps, warp_weights)
        unused, agg_vjp = jax.vjp(lambda first, second: aggregate(first, second, view_gate), ref_map, warped)
        ref_grad, warp_grad = agg_vjp(cost_grad[index])
        warp_round = lax.optimization_barrier(warp_grad.astype(jnp.bfloat16))
        src_grad = jnp.einsum('sdcx,dxy->scy', warp_round.astype(jnp.float32), warp_weights.astype(jnp.float32), precision=lax.Precision.HIGHEST)
        return (ref_grad, src_grad)
    ref_grad, src_grad = lax.map(backward_one, jnp.arange(NV))
    summed = jax.ops.segment_sum(src_grad.reshape(NV * S, C, PIX), sources.reshape(NV * S), num_segments=NV)
    return (regular, ref_grad + summed)
```

```python
import functools

import jax
import jax.numpy as jnp
from jax import lax
from jax.experimental import pallas as pl
from jax.experimental.pallas import tpu as pltpu
from jax.sharding import PartitionSpec as P

G = 8
GC = 4
C = G * GC


def extended(cells, sides, width):
    for axis, dim in sides:
        count = lax.axis_size(axis)
        ends = count - 1
        head = lax.slice_in_dim(cells, 0, width, axis=dim)
        tail = lax.slice_in_dim(cells, cells.shape[dim] - width, cells.shape[dim], axis=dim)
        cells = jnp.concatenate(
            [
                lax.ppermute(tail, axis, [(i, (i + 1) % count) for i in range(ends)]),
                cells,
                lax.ppermute(head, axis, [((i + 1) % count, i) for i in range(ends)]),
            ],
            axis=dim,
        )
    return cells


def group_minor(maps):
    lead, pixels = maps.shape[:-2], maps.shape[-1]
    return maps.reshape(lead + (G, GC, pixels)).swapaxes(-3, -2).reshape(maps.shape)


def group_major(maps):
    lead, pixels = maps.shape[:-2], maps.shape[-1]
    return maps.reshape(lead + (GC, G, pixels)).swapaxes(-3, -2).reshape(maps.shape)


def fwd_kernel(views, per_view, tiles_ref, refs_ref, w_ref, gate_ref, warped_ref, corr_ref, aux_ref, cost_ref):
    gate = gate_ref[...] * 0.125
    pixels = w_ref.shape[1]
    gate_b = jnp.broadcast_to(gate, (G, pixels))
    rows = per_view * C
    for r in range(views):
        warped = lax.dot_general(
            tiles_ref[r * rows : (r + 1) * rows, :],
            w_ref[0],
            (((1,), (1,)), ((), ())),
            preferred_element_type=jnp.float32,
        )
        warped_ref[0, r] = warped.astype(jnp.bfloat16)
        ref_map = refs_ref[r].astype(jnp.float32)
        weighted = None
        for s in range(per_view):
            product = warped[s * C : (s + 1) * C] * ref_map
            corr = (product[0:8] + product[8:16]) + (product[16:24] + product[24:32])
            corr_ref[0, r, s * G : (s + 1) * G, :] = corr
            half = jnp.sum(corr * gate_b, axis=0, keepdims=True)
            turn = jnp.tanh(half)
            aux_ref[0, r, s : s + 1, :] = turn
            visible = 1.0 + 0.5 * turn
            if weighted is None:
                weighted = visible * corr
                total = visible
            else:
                weighted = weighted + visible * corr
                total = total + visible
        inverse = 1.0 / total
        aux_ref[0, r, per_view : per_view + 1, :] = inverse
        cost_ref[0, r] = weighted * (inverse * 0.25)


def forward(tiles, refs, warp_weights, gate):
    planes, pixels, _ = warp_weights.shape
    views = refs.shape[0]
    per_view = tiles.shape[0] // (views * C)
    rows = per_view * C
    f32, bf16 = jnp.float32, jnp.bfloat16
    return pl.pallas_call(
        functools.partial(fwd_kernel, views, per_view),
        grid=(planes,),
        in_specs=[
            pl.BlockSpec(tiles.shape, lambda d: (0, 0)),
            pl.BlockSpec(refs.shape, lambda d: (0, 0, 0)),
            pl.BlockSpec((1, pixels, pixels), lambda d: (d, 0, 0)),
            pl.BlockSpec((G, 1), lambda d: (0, 0)),
        ],
        out_specs=[
            pl.BlockSpec((1, views, rows, pixels), lambda d: (d, 0, 0, 0)),
            pl.BlockSpec((1, views, per_view * G, pixels), lambda d: (d, 0, 0, 0)),
            pl.BlockSpec((1, views, 16, pixels), lambda d: (d, 0, 0, 0)),
            pl.BlockSpec((1, views, G, pixels), lambda d: (d, 0, 0, 0)),
        ],
        out_shape=[
            jax.ShapeDtypeStruct((planes, views, rows, pixels), bf16),
            jax.ShapeDtypeStruct((planes, views, per_view * G, pixels), f32),
            jax.ShapeDtypeStruct((planes, views, 16, pixels), f32),
            jax.ShapeDtypeStruct((planes, views, G, pixels), f32),
        ],
        compiler_params=pltpu.CompilerParams(dimension_semantics=("arbitrary",)),
        name="warp_forward",
    )(tiles, refs, warp_weights, gate)


def bwd_kernel(views, per_view, warped_ref, corr_ref, aux_ref, cost_ref, grad_ref, refs_ref, w_ref, gate_ref, src_ref, own_ref, slab_ref):
    gate = gate_ref[...] * 0.0625
    pixels = w_ref.shape[1]
    gate_b = jnp.broadcast_to(gate, (G, pixels))
    rows = per_view * C

    @pl.when(pl.program_id(0) == 0)
    def _():
        src_ref[...] = jnp.zeros_like(src_ref)
        own_ref[...] = jnp.zeros_like(own_ref)

    for r in range(views):
        ref_map = refs_ref[r].astype(jnp.float32)
        inverse = aux_ref[0, r, per_view : per_view + 1, :]
        d_num = grad_ref[0, r] * (inverse * 0.25)
        cost4 = cost_ref[0, r] * 4.0
        own = None
        for s in range(per_view):
            corr = corr_ref[0, r, s * G : (s + 1) * G, :]
            turn = aux_ref[0, r, s : s + 1, :]
            push = jnp.sum(d_num * (corr - cost4), axis=0, keepdims=True)
            push = push * (1.0 - turn * turn)
            d_corr = d_num * (1.0 + 0.5 * turn) + gate_b * push
            d_tile = jnp.concatenate([d_corr] * GC, axis=0)
            slab_ref[r, s * C : (s + 1) * C, :] = (d_tile * ref_map).astype(jnp.bfloat16)
            part = d_tile * warped_ref[0, r, s * C : (s + 1) * C, :].astype(jnp.float32)
            own = part if own is None else own + part
        own_ref[r] += own
        src_ref[r * rows : (r + 1) * rows, :] += jnp.dot(
            slab_ref[r], w_ref[0], preferred_element_type=jnp.float32
        )


def backward(warped, corr, aux, cost, cost_grad, refs, warp_weights, gate):
    planes, pixels, _ = warp_weights.shape
    views = refs.shape[0]
    rows = warped.shape[2]
    per_view = rows // C
    f32, bf16 = jnp.float32, jnp.bfloat16
    return pl.pallas_call(
        functools.partial(bwd_kernel, views, per_view),
        grid=(planes,),
        in_specs=[
            pl.BlockSpec((1, views, rows, pixels), lambda d: (d, 0, 0, 0)),
            pl.BlockSpec((1, views, per_view * G, pixels), lambda d: (d, 0, 0, 0)),
            pl.BlockSpec((1, views, 16, pixels), lambda d: (d, 0, 0, 0)),
            pl.BlockSpec((1, views, G, pixels), lambda d: (d, 0, 0, 0)),
            pl.BlockSpec((1, views, G, pixels), lambda d: (d, 0, 0, 0)),
            pl.BlockSpec(refs.shape, lambda d: (0, 0, 0)),
            pl.BlockSpec((1, pixels, pixels), lambda d: (d, 0, 0)),
            pl.BlockSpec((G, 1), lambda d: (0, 0)),
        ],
        out_specs=[
            pl.BlockSpec((views * rows, pixels), lambda d: (0, 0)),
            pl.BlockSpec((views, C, pixels), lambda d: (0, 0, 0)),
        ],
        out_shape=[
            jax.ShapeDtypeStruct((views * rows, pixels), f32),
            jax.ShapeDtypeStruct((views, C, pixels), f32),
        ],
        scratch_shapes=[pltpu.VMEM((views, rows, pixels), bf16)],
        compiler_params=pltpu.CompilerParams(dimension_semantics=("arbitrary",)),
        name="warp_backward",
    )(warped, corr, aux, cost, cost_grad, refs, warp_weights, gate)


def shards(features, sources, warp_weights, view_gate, depth_kernel, cotangent):
    view_count = lax.axis_size("view")
    own_index = lax.axis_index("view")
    local_views, channels, pixels = features.shape
    per_view = sources.shape[1]
    requests = local_views * per_view
    capacity = max(2, (2 * requests + view_count - 1) // view_count)
    planes = warp_weights.shape[0]
    highest = lax.Precision.HIGHEST
    mine_req = lax.dynamic_slice_in_dim(sources, own_index * local_views, local_views, 0).reshape(
        requests
    )
    owner_req = mine_req // local_views
    positions = jnp.arange(requests)
    earlier = (owner_req[None, :] == owner_req[:, None]) & (positions[None, :] < positions[:, None])
    rank_req = jnp.sum(earlier.astype(jnp.int32), axis=1)
    slot_id = owner_req * capacity + rank_req
    picker = (slot_id[:, None] == jnp.arange(view_count * capacity)[None, :]).astype(jnp.bfloat16)
    all_req = sources.reshape(view_count, requests)
    mine_mask = all_req // local_views == own_index
    rank_all = jnp.cumsum(mine_mask.astype(jnp.int32), axis=1) - 1
    slot_hit = (
        mine_mask[:, :, None] & (rank_all[:, :, None] == jnp.arange(capacity)[None, None, :])
    ).astype(jnp.float32)
    local_hit = (
        (all_req % local_views)[:, :, None] == jnp.arange(local_views)[None, None, :]
    ).astype(jnp.float32)
    selector = jnp.einsum("pjk,pjl->pkl", slot_hit, local_hit, precision=highest)
    outgoing = jnp.einsum(
        "pkl,lcx->pkcx", selector.astype(jnp.bfloat16), features, preferred_element_type=jnp.float32
    ).astype(jnp.bfloat16)
    incoming = lax.all_to_all(outgoing, "view", split_axis=0, concat_axis=0, tiled=True)
    gathered = jnp.einsum(
        "jn,ncx->jcx",
        picker,
        incoming.reshape(view_count * capacity, channels, pixels),
        preferred_element_type=jnp.float32,
    ).astype(jnp.bfloat16)
    source_tiles = gathered.reshape(local_views, per_view, channels, pixels)

    refs = group_minor(features)
    gate = view_gate.reshape(G, 1)
    tiles = group_minor(source_tiles).reshape(requests * channels, pixels)
    warped, corr, aux, cost = forward(tiles, refs, warp_weights, gate)
    cost_volume = cost.swapaxes(0, 1)
    padded = extended(cost_volume, (("plane", 1),), 1)
    pre_act = jnp.zeros(cost_volume.shape, jnp.float32)
    for offset in range(3):
        pre_act = pre_act + jnp.einsum(
            "og,rdgx->rdox",
            depth_kernel[offset],
            padded[:, offset : offset + planes],
            precision=highest,
        )
    regular = jax.nn.silu(pre_act).astype(jnp.bfloat16)
    sigmoid_pre = jax.nn.sigmoid(pre_act)
    pre_grad = cotangent.astype(jnp.float32) * (sigmoid_pre * (1.0 + pre_act * (1.0 - sigmoid_pre)))
    padded_slope = extended(pre_grad, (("plane", 1),), 1)
    cost_grad = jnp.zeros(cost_volume.shape, jnp.float32)
    for offset in range(3):
        cost_grad = cost_grad + jnp.einsum(
            "og,rdox->rdgx",
            depth_kernel[offset],
            padded_slope[:, 2 - offset : 2 - offset + planes],
            precision=highest,
        )

    src_grad, ref_grad = backward(
        warped, corr, aux, cost, cost_grad.swapaxes(0, 1), refs, warp_weights, gate
    )
    ref_grad = group_major(ref_grad)
    src_grad = group_major(src_grad.reshape(requests, channels, pixels))
    src_grad, ref_grad = lax.psum((src_grad, ref_grad), "plane")
    flat_grad = src_grad.reshape(requests, channels, pixels)
    outbound = jnp.einsum("jn,jcx->ncx", picker.astype(jnp.float32), flat_grad, precision=highest)
    inbound = lax.all_to_all(
        outbound.reshape(view_count, capacity, channels, pixels).astype(jnp.bfloat16),
        "view",
        split_axis=0,
        concat_axis=0,
        tiled=True,
    ).astype(jnp.float32)
    returned = jnp.einsum("pkl,pkcx->lcx", selector, inbound, precision=highest)
    owner_sum = ref_grad + returned
    return (regular, owner_sum)


def solution(mesh):
    in_specs = (
        P("view", None, None),
        P(),
        P("plane", None, None),
        P(),
        P(),
        P("view", "plane", None, None),
    )
    out_specs = (P("view", "plane", None, None), P("view", None, None))
    return jax.shard_map(shards, mesh=mesh, in_specs=in_specs, out_specs=out_specs, check_vma=False)
```

```python
import functools

import jax
import jax.numpy as jnp
from jax import lax
from jax.experimental import pallas as pl
from jax.experimental.pallas import tpu as pltpu
from jax.sharding import PartitionSpec as P

G = 8
GC = 4
C = G * GC
LANES = 128
MESH = pl.DeviceIdType.MESH
f32 = jnp.float32
bf16 = jnp.bfloat16


def column(row):
    eye = lax.broadcasted_iota(jnp.int32, (G, G), 0) == lax.broadcasted_iota(jnp.int32, (G, G), 1)
    return jnp.sum(jnp.where(eye, jnp.broadcast_to(row, (G, G)), 0.0), axis=1, keepdims=True)


def greet(peers):
    barrier = pltpu.get_barrier_semaphore()
    for peer in peers:
        pl.semaphore_signal(barrier, inc=1, device_id=peer, device_id_type=MESH)
    pl.semaphore_wait(barrier, len(peers))


def gather_kernel(
    views, per_view, n_view, n_plane, feat_ref, sources_ref, tiles_ref, refs_ref, quarter, ring_send, ring_recv, pair_send, pair_recv, line_send, line_recv
):
    v, p = lax.axis_index("view"), lax.axis_index("plane")
    sibling = v + 1 - 2 * lax.rem(v, 2)
    chips = n_view // 2
    lanes = pl.ds(pl.multiple_of(p * LANES, LANES), LANES)

    into = lax.broadcasted_iota(jnp.int32, (C, C), 0)
    outof = lax.broadcasted_iota(jnp.int32, (C, C), 1)
    swap = (outof == (into % G) * GC + into // G).astype(bf16)
    for i in range(views):
        refs_ref[i] = jnp.dot(swap, feat_ref[i], preferred_element_type=f32).astype(bf16)
    quarter[pl.ds(v * views, views)] = refs_ref[:, :, lanes]

    peers = [(lax.rem(v + 2 * j, n_view), p) for j in range(1, chips)]
    peers += [(sibling, p)]
    peers += [(v, lax.rem(p + j, n_plane)) for j in range(1, n_plane)]
    greet(peers)

    def ring_copy(j, owner, target):
        block = quarter.at[pl.ds(owner * views, views)]
        return pltpu.make_async_remote_copy(
            src_ref=block, dst_ref=block, send_sem=ring_send.at[j], recv_sem=ring_recv.at[j],
            device_id=(target, p), device_id_type=MESH)

    def pair_copy(j, owner):
        block = quarter.at[pl.ds(owner * views, views)]
        return pltpu.make_async_remote_copy(
            src_ref=block, dst_ref=block, send_sem=pair_send.at[j], recv_sem=pair_recv.at[j],
            device_id=(sibling, p), device_id_type=MESH)

    @pl.loop(1, chips)
    def _(j):
        ring_copy(j, v, lax.rem(v + 2 * j, n_view)).start()

    pair_copy(0, v).start()

    @pl.loop(1, chips)
    def _(j):
        owner = lax.rem(v - 2 * j + n_view, n_view)
        ring_copy(j, owner, owner).wait_recv()
        pair_copy(j, owner).start()

    @pl.loop(0, chips)
    def _(j):
        pair_copy(j, lax.rem(sibling - 2 * j + n_view, n_view)).wait_recv()

    def line_copy(r, j):
        rows = pl.ds(r * per_view * C, per_view * C)
        block = tiles_ref.at[rows, lanes]
        return pltpu.make_async_remote_copy(
            src_ref=block, dst_ref=block, send_sem=line_send.at[r, j - 1], recv_sem=line_recv.at[r, j - 1],
            device_id=(v, lax.rem(p + j, n_plane)), device_id_type=MESH)

    def arrived(r, j):
        rows = pl.ds(r * per_view * C, per_view * C)
        other = lax.rem(p - j + n_plane, n_plane)
        block = tiles_ref.at[rows, pl.ds(pl.multiple_of(other * LANES, LANES), LANES)]
        return pltpu.make_async_remote_copy(
            src_ref=block, dst_ref=block, send_sem=line_send.at[r, j - 1], recv_sem=line_recv.at[r, j - 1],
            device_id=(v, other), device_id_type=MESH)

    for r in range(views):

        @pl.loop(0, per_view)
        def _(s):
            source = sources_ref[v * views + r, s]
            start = pl.multiple_of((r * per_view + s) * C, C)
            tiles_ref[pl.ds(start, C), lanes] = quarter[source]

        if r > 0:
            for j in range(1, n_plane):
                line_copy(r - 1, j).start()

    @pl.loop(1, chips)
    def _(j):
        ring_copy(j, v, lax.rem(v + 2 * j, n_view)).wait_send()

    for j in range(1, n_plane):
        line_copy(views - 1, j).start()

    @pl.loop(0, chips)
    def _(j):
        pair_copy(j, lax.rem(v - 2 * j + n_view, n_view)).wait_send()

    for r in range(views):
        for j in range(1, n_plane):
            line_copy(r, j).wait_send()
            arrived(r, j).wait_recv()


def gather(features, sources, n_view, n_plane):
    views, channels, pixels = features.shape
    per_view = sources.shape[1]
    chips = n_view // 2
    dma = pltpu.SemaphoreType.DMA
    return pl.pallas_call(
        functools.partial(gather_kernel, views, per_view, n_view, n_plane),
        in_specs=[pl.BlockSpec(memory_space=pltpu.VMEM), pl.BlockSpec(memory_space=pltpu.SMEM)],
        out_specs=[pl.BlockSpec(memory_space=pltpu.VMEM)] * 2,
        out_shape=[
            jax.ShapeDtypeStruct((views * per_view * channels, pixels), bf16),
            jax.ShapeDtypeStruct((views, channels, pixels), bf16),
        ],
        scratch_shapes=[
            pltpu.VMEM((n_view * views, channels, LANES), bf16),
            dma((chips,)), dma((chips,)), dma((chips,)), dma((chips,)),
            dma((views, n_plane - 1)), dma((views, n_plane - 1)),
        ],
        compiler_params=pltpu.CompilerParams(collective_id=0, has_side_effects=True),
        name="gather_maps",
    )(features, sources)


def fwd_kernel(views, per_view, tiles_ref, refs_ref, w_ref, gate_ref, warped_ref, corr_ref, aux_ref, cost_ref):
    pixels = w_ref.shape[1]
    gate_b = jnp.broadcast_to(column(gate_ref[...] * 0.125), (G, pixels))
    rows = per_view * C
    for r in range(views):
        warped = lax.dot_general(
            tiles_ref[r * rows : (r + 1) * rows, :],
            w_ref[0],
            (((1,), (1,)), ((), ())),
            preferred_element_type=f32,
        )
        warped_ref[0, r] = warped.astype(bf16)
        ref_map = refs_ref[r].astype(f32)
        weighted = None
        for s in range(per_view):
            product = warped[s * C : (s + 1) * C] * ref_map
            corr = (product[0:8] + product[8:16]) + (product[16:24] + product[24:32])
            corr_ref[0, r, s * G : (s + 1) * G, :] = corr
            half = jnp.sum(corr * gate_b, axis=0, keepdims=True)
            turn = jnp.tanh(half)
            aux_ref[0, r, s : s + 1, :] = turn
            visible = 1.0 + 0.5 * turn
            if weighted is None:
                weighted = visible * corr
                total = visible
            else:
                weighted = weighted + visible * corr
                total = total + visible
        inverse = 1.0 / total
        aux_ref[0, r, per_view : per_view + 1, :] = inverse
        cost_ref[0, r] = weighted * (inverse * 0.25)


def forward(tiles, refs, warp_weights, gate):
    planes, pixels, _ = warp_weights.shape
    views = refs.shape[0]
    per_view = tiles.shape[0] // (views * C)
    rows = per_view * C
    return pl.pallas_call(
        functools.partial(fwd_kernel, views, per_view),
        grid=(planes,),
        in_specs=[
            pl.BlockSpec(tiles.shape, lambda d: (0, 0)),
            pl.BlockSpec(refs.shape, lambda d: (0, 0, 0)),
            pl.BlockSpec((1, pixels, pixels), lambda d: (d, 0, 0)),
            pl.BlockSpec((1, G), lambda d: (0, 0)),
        ],
        out_specs=[
            pl.BlockSpec((1, views, rows, pixels), lambda d: (d, 0, 0, 0)),
            pl.BlockSpec((1, views, per_view * G, pixels), lambda d: (d, 0, 0, 0)),
            pl.BlockSpec((1, views, 16, pixels), lambda d: (d, 0, 0, 0)),
            pl.BlockSpec((1, views, G, pixels), lambda d: (d, 0, 0, 0)),
        ],
        out_shape=[
            jax.ShapeDtypeStruct((planes, views, rows, pixels), bf16),
            jax.ShapeDtypeStruct((planes, views, per_view * G, pixels), f32),
            jax.ShapeDtypeStruct((planes, views, 16, pixels), f32),
            jax.ShapeDtypeStruct((planes, views, G, pixels), f32),
        ],
        compiler_params=pltpu.CompilerParams(dimension_semantics=("arbitrary",)),
        name="warp_forward",
    )(tiles, refs, warp_weights, gate)


def depth_kernel_body(views, planes, n_plane, cost_ref, taps_ref, cot_ref, grad_ref, regular_ref, cost_ext, slope_ext, taps_fwd, taps_bwd, cost_send, cost_recv, slope_send, slope_recv):
    v, p = lax.axis_index("view"), lax.axis_index("plane")
    left = (v, lax.rem(p + n_plane - 1, n_plane))
    right = (v, lax.rem(p + 1, n_plane))

    def edges(buffer, send, recv):
        return (
            pltpu.make_async_remote_copy(
                src_ref=buffer.at[1], dst_ref=buffer.at[planes + 1], send_sem=send.at[0],
                recv_sem=recv.at[0], device_id=left, device_id_type=MESH),
            pltpu.make_async_remote_copy(
                src_ref=buffer.at[planes], dst_ref=buffer.at[0], send_sem=send.at[1],
                recv_sem=recv.at[1], device_id=right, device_id_type=MESH),
        )

    cost_ext[1] = cost_ref[0]
    cost_ext[planes] = cost_ref[planes - 1]
    pixels = cost_ref.shape[-1]
    for k in range(3):
        taps = taps_ref[k]
        for g in range(G):
            taps_fwd[k * G + g] = jnp.broadcast_to(taps[:, g : g + 1], (G, LANES))
            taps_bwd[k * G + g] = jnp.broadcast_to(column(taps[g : g + 1, :]), (G, LANES))
    greet([left, right])
    first = edges(cost_ext, cost_send, cost_recv)
    for copy in first:
        copy.start()

    @pl.loop(1, planes - 1)
    def _(d):
        cost_ext[d + 1] = cost_ref[d]

    def conv(buffer, taps, r, d, flip):
        total = [None] * (pixels // LANES)
        for k in range(3):
            at = d + (2 - k if flip else k)
            for g in range(G):
                tap = taps[k * G + g]
                for t in range(pixels // LANES):
                    row = buffer[at, r, g : g + 1, t * LANES : (t + 1) * LANES]
                    term = tap * jnp.broadcast_to(row, (G, LANES))
                    total[t] = term if total[t] is None else total[t] + term
        return jnp.concatenate(total, axis=1)

    def activate(r, d):
        pre = conv(cost_ext, taps_fwd, r, d, False)
        gate = jax.nn.sigmoid(pre)
        regular_ref[r, d] = (pre * gate).astype(bf16)
        slope_ext[d + 1, r] = cot_ref[r, d].astype(f32) * (gate * (1.0 + pre * (1.0 - gate)))

    def over_views(body, d):
        @pl.loop(0, views)
        def _(r):
            body(r, d)

    @pl.loop(1, planes - 1)
    def _(d):
        over_views(activate, d)

    def mask(buffer):
        inner_left = jnp.where(p == 0, 0.0, 1.0)
        inner_right = jnp.where(p == n_plane - 1, 0.0, 1.0)
        buffer[0] = buffer[0] * inner_left
        buffer[planes + 1] = buffer[planes + 1] * inner_right

    for copy in first:
        copy.wait()
    mask(cost_ext)
    over_views(activate, 0)
    over_views(activate, planes - 1)

    def push(r, d):
        grad_ref[d, r] = conv(slope_ext, taps_bwd, r, d, True)

    over_views(push, 1)
    second = edges(slope_ext, slope_send, slope_recv)
    for copy in second:
        copy.start()

    @pl.loop(2, planes - 1)
    def _(d):
        over_views(push, d)

    for copy in second:
        copy.wait()
    mask(slope_ext)
    over_views(push, 0)
    over_views(push, planes - 1)


def regularize(cost, taps, cotangent, n_plane):
    planes, views, groups, pixels = cost.shape
    dma = pltpu.SemaphoreType.DMA
    return pl.pallas_call(
        functools.partial(depth_kernel_body, views, planes, n_plane),
        in_specs=[pl.BlockSpec(memory_space=pltpu.VMEM)] * 3,
        out_specs=[pl.BlockSpec(memory_space=pltpu.VMEM)] * 2,
        out_shape=[
            jax.ShapeDtypeStruct(cost.shape, f32),
            jax.ShapeDtypeStruct((views, planes, groups, pixels), bf16),
        ],
        scratch_shapes=[
            pltpu.VMEM((planes + 2, views, groups, pixels), f32),
            pltpu.VMEM((planes + 2, views, groups, pixels), f32),
            pltpu.VMEM((3 * G, G, LANES), f32),
            pltpu.VMEM((3 * G, G, LANES), f32),
            dma((2,)), dma((2,)), dma((2,)), dma((2,)),
        ],
        compiler_params=pltpu.CompilerParams(collective_id=1, has_side_effects=True),
        name="regularize_depth",
    )(cost, taps, cotangent)


def bwd_kernel(views, per_view, planes, warped_ref, corr_ref, aux_ref, cost_ref, grad_ref, refs_ref, w_ref, gate_ref, regular_ref, use_ref, out_ref, src_acc, own_acc, slab_ref):
    pixels = w_ref.shape[1]
    gate_b = jnp.broadcast_to(column(gate_ref[...] * 0.0625), (G, pixels))
    rows = per_view * C
    out_ref[...] = regular_ref[...]

    @pl.when(pl.program_id(0) == 0)
    def _():
        src_acc[...] = jnp.zeros_like(src_acc)
        own_acc[...] = jnp.zeros_like(own_acc)

    for r in range(views):
        ref_map = refs_ref[r].astype(f32)
        inverse = aux_ref[0, r, per_view : per_view + 1, :]
        d_num = grad_ref[0, r] * (inverse * 0.25)
        cost4 = cost_ref[0, r] * 4.0
        own = None
        for s in range(per_view):
            corr = corr_ref[0, r, s * G : (s + 1) * G, :]
            turn = aux_ref[0, r, s : s + 1, :]
            push = jnp.sum(d_num * (corr - cost4), axis=0, keepdims=True)
            push = push * (1.0 - turn * turn)
            d_corr = d_num * (1.0 + 0.5 * turn) + gate_b * push
            d_tile = jnp.concatenate([d_corr] * GC, axis=0)
            slab_ref[r, s * C : (s + 1) * C, :] = (d_tile * ref_map).astype(bf16)
            part = d_tile * warped_ref[0, r, s * C : (s + 1) * C, :].astype(f32)
            own = part if own is None else own + part
        own_acc[r * C : (r + 1) * C] += own
        src_acc[r * rows : (r + 1) * rows, :] += jnp.dot(slab_ref[r], w_ref[0], preferred_element_type=f32)

    @pl.when(pl.program_id(0) == planes - 1)
    def _():
        use_ref[0 : views * rows] = src_acc[...].astype(bf16)
        use_ref[views * rows :] = own_acc[...].astype(bf16)


def backward(warped, corr, aux, cost, cost_grad, refs, warp_weights, gate, regular):
    planes, pixels, _ = warp_weights.shape
    views = refs.shape[0]
    rows = warped.shape[2]
    per_view = rows // C
    return pl.pallas_call(
        functools.partial(bwd_kernel, views, per_view, planes),
        grid=(planes,),
        in_specs=[
            pl.BlockSpec((1, views, rows, pixels), lambda d: (d, 0, 0, 0)),
            pl.BlockSpec((1, views, per_view * G, pixels), lambda d: (d, 0, 0, 0)),
            pl.BlockSpec((1, views, 16, pixels), lambda d: (d, 0, 0, 0)),
            pl.BlockSpec((1, views, G, pixels), lambda d: (d, 0, 0, 0)),
            pl.BlockSpec((1, views, G, pixels), lambda d: (d, 0, 0, 0)),
            pl.BlockSpec(refs.shape, lambda d: (0, 0, 0)),
            pl.BlockSpec((1, pixels, pixels), lambda d: (d, 0, 0)),
            pl.BlockSpec((1, G), lambda d: (0, 0)),
            pl.BlockSpec((views, 1, G, pixels), lambda d: (0, d, 0, 0)),
        ],
        out_specs=[
            pl.BlockSpec((views * (rows + C), pixels), lambda d: (0, 0)),
            pl.BlockSpec((views, 1, G, pixels), lambda d: (0, d, 0, 0)),
        ],
        out_shape=[
            jax.ShapeDtypeStruct((views * (rows + C), pixels), bf16),
            jax.ShapeDtypeStruct(regular.shape, bf16),
        ],
        scratch_shapes=[
            pltpu.VMEM((views * rows, pixels), f32),
            pltpu.VMEM((views * C, pixels), f32),
            pltpu.VMEM((views, rows, pixels), bf16),
        ],
        compiler_params=pltpu.CompilerParams(dimension_semantics=("arbitrary",)),
        name="warp_backward",
    )(warped, corr, aux, cost, cost_grad, refs, warp_weights, gate, regular)


def scatter_kernel(
    views, per_view, n_view, n_plane, use_ref, sources_ref, out_ref, line_in, summed, paired, dense, blocks, ring_in, result, ordered, line_send, line_recv, pair_send, pair_recv, ring_send, ring_recv, last_send, last_recv
):
    v, p = lax.axis_index("view"), lax.axis_index("plane")
    core = lax.rem(v, 2)
    chip = v // 2
    sibling = v + 1 - 2 * core
    chips = n_view // 2
    uses = views * (per_view + 1)
    block = views * C

    def lanes(q):
        return pl.ds(pl.multiple_of(q * LANES, LANES), LANES)

    peers = [(lax.rem(v + 2 * j, n_view), p) for j in range(1, chips)]
    peers += [(sibling, p)]
    peers += [(v, lax.rem(p + j, n_plane)) for j in range(1, n_plane)]
    greet(peers)

    line = []
    for j in range(1, n_plane):
        target = lax.rem(p + j, n_plane)
        line.append(
            pltpu.make_async_remote_copy(
                src_ref=use_ref.at[:, lanes(target)], dst_ref=line_in.at[j - 1], send_sem=line_send.at[j - 1],
                recv_sem=line_recv.at[j - 1], device_id=(v, target), device_id_type=MESH))
        line[-1].start()

    place = lax.broadcasted_iota(jnp.int32, (1, LANES), 1)
    named = jnp.full((1, LANES), -1, jnp.int32)
    for half, device in enumerate((v, sibling)):
        for r in range(views):
            for s in range(per_view):
                named = jnp.where(place == half * 64 + r * per_view + s, sources_ref[device * views + r, s], named)
            named = jnp.where(place == half * 64 + views * per_view + r, device * views + r, named)
    row = lax.broadcasted_iota(jnp.int32, (chips * views, LANES), 0)
    goal = (row // views) * (2 * views) + core * views + row % views
    pick = (goal == jnp.broadcast_to(named, (chips * views, LANES))).astype(bf16)

    for copy in line:
        copy.wait_recv()
    own = use_ref[:, lanes(p)].astype(f32)
    summed[...] = own + ((line_in[0].astype(f32) + line_in[1].astype(f32)) + line_in[2].astype(f32))
    for copy in line:
        copy.wait_send()
    pair = pltpu.make_async_remote_copy(
        src_ref=summed, dst_ref=paired, send_sem=pair_send, recv_sem=pair_recv,
        device_id=(sibling, p), device_id_type=MESH)
    pair.start()
    pair.wait()

    gap = jnp.zeros((64 - uses, LANES), f32)

    @pl.loop(0, C)
    def _(c):
        stack = jnp.concatenate(
            [summed[pl.ds(c, uses, stride=C), :], gap, paired[pl.ds(c, uses, stride=C), :], gap], axis=0)
        high = stack.astype(bf16)
        low = (stack - high.astype(f32)).astype(bf16)
        dense[pl.ds(c, chips * views, stride=C), :] = jnp.dot(pick, high, preferred_element_type=f32) + jnp.dot(
            pick, low, preferred_element_type=f32)

    def ring_copy(j, target, origin):
        return pltpu.make_async_remote_copy(
            src_ref=blocks.at[target], dst_ref=ring_in.at[origin], send_sem=ring_send.at[j], recv_sem=ring_recv.at[j],
            device_id=(2 * target + core, p), device_id_type=MESH)

    def shift(j):
        return lax.rem(chip + j, chips)

    @pl.loop(1, chips)
    def _(j):
        start = pl.multiple_of(shift(j) * block, block)
        blocks[shift(j)] = dense[pl.ds(start, block), :].astype(bf16)

        @pl.when(j > 1)
        def _():
            ring_copy(j - 1, shift(j - 1), chip).start()

    result[...] = dense[pl.ds(pl.multiple_of(chip * block, block), block), :]
    ring_copy(chips - 1, shift(chips - 1), chip).start()

    @pl.loop(1, chips)
    def _(j):
        origin = lax.rem(chip - j + chips, chips)
        ring_copy(j, chip, origin).wait_recv()
        result[...] += ring_in[origin].astype(f32)

    for i in range(views):
        for k in range(GC):
            ordered[pl.ds(i * C + k, G, stride=GC), :] = result[i * C + k * G : i * C + (k + 1) * G, :]
        out_ref[i, :, lanes(p)] = ordered[i * C : (i + 1) * C, :]

    @pl.loop(1, chips)
    def _(j):
        ring_copy(j, shift(j), chip).wait_send()

    def last_copy(j, q, target):
        part = out_ref.at[:, :, lanes(q)]
        return pltpu.make_async_remote_copy(
            src_ref=part, dst_ref=part, send_sem=last_send.at[j - 1], recv_sem=last_recv.at[j - 1],
            device_id=(v, target), device_id_type=MESH)

    for j in range(1, n_plane):
        last_copy(j, p, lax.rem(p + j, n_plane)).start()
    for j in range(1, n_plane):
        other = lax.rem(p - j + n_plane, n_plane)
        last_copy(j, p, lax.rem(p + j, n_plane)).wait_send()
        last_copy(j, other, other).wait_recv()


def scatter(uses, sources, views, n_view, n_plane):
    rows, pixels = uses.shape
    per_view = sources.shape[1]
    chips = n_view // 2
    dma = pltpu.SemaphoreType.DMA
    return pl.pallas_call(
        functools.partial(scatter_kernel, views, per_view, n_view, n_plane),
        in_specs=[pl.BlockSpec(memory_space=pltpu.VMEM), pl.BlockSpec(memory_space=pltpu.SMEM)],
        out_specs=pl.BlockSpec(memory_space=pltpu.VMEM),
        out_shape=jax.ShapeDtypeStruct((views, C, pixels), f32),
        scratch_shapes=[
            pltpu.VMEM((n_plane - 1, rows, LANES), bf16),
            pltpu.VMEM((rows, LANES), f32),
            pltpu.VMEM((rows, LANES), f32),
            pltpu.VMEM((chips * views * C, LANES), f32),
            pltpu.VMEM((chips, views * C, LANES), bf16),
            pltpu.VMEM((chips, views * C, LANES), bf16),
            pltpu.VMEM((views * C, LANES), f32),
            pltpu.VMEM((views * C, LANES), f32),
            dma((n_plane - 1,)), dma((n_plane - 1,)),
            dma, dma,
            dma((chips,)), dma((chips,)),
            dma((n_plane - 1,)), dma((n_plane - 1,)),
        ],
        compiler_params=pltpu.CompilerParams(collective_id=2, has_side_effects=True),
        name="scatter_grads",
    )(uses, sources)


def shards(n_view, n_plane, features, sources, warp_weights, view_gate, depth_kernel, cotangent):
    views = features.shape[0]
    gate = view_gate.reshape(1, G)
    tiles, refs = gather(features, sources, n_view, n_plane)
    warped, corr, aux, cost = forward(tiles, refs, warp_weights, gate)
    cost_grad, regular = regularize(cost, depth_kernel, cotangent, n_plane)
    uses, regular = backward(warped, corr, aux, cost, cost_grad, refs, warp_weights, gate, regular)
    grads = scatter(uses, sources, views, n_view, n_plane)
    return regular, grads


def solution(mesh):
    in_specs = (
        P("view", None, None),
        P(),
        P("plane", None, None),
        P(),
        P(),
        P("view", "plane", None, None),
    )
    out_specs = (P("view", "plane", None, None), P("view", None, None))
    body = functools.partial(shards, mesh.shape["view"], mesh.shape["plane"])
    return jax.shard_map(body, mesh=mesh, in_specs=in_specs, out_specs=out_specs, check_vma=False)
```

```python
import functools

import jax
import jax.numpy as jnp
from jax import lax
from jax.experimental import pallas as pl
from jax.experimental.pallas import tpu as pltpu
from jax.sharding import PartitionSpec as P

G = 8
GC = 4
C = G * GC
LANES = 128
MESH = pl.DeviceIdType.MESH
f32 = jnp.float32
bf16 = jnp.bfloat16


def column(row):
    eye = lax.broadcasted_iota(jnp.int32, (G, G), 0) == lax.broadcasted_iota(jnp.int32, (G, G), 1)
    return jnp.sum(jnp.where(eye, jnp.broadcast_to(row, (G, G)), 0.0), axis=1, keepdims=True)


def greet(peers):
    barrier = pltpu.get_barrier_semaphore()
    for peer in peers:
        pl.semaphore_signal(barrier, inc=1, device_id=peer, device_id_type=MESH)
    pl.semaphore_wait(barrier, len(peers))


def sweep_kernel(
    dims,
    feat_ref, sources_ref, w_hbm, gate_ref, taps_ref, cot_ref,
    regular_ref, out_ref,
    w_ref, refs_ref, quarter, tiles_ref, warped_ref, corr_ref, aux_ref, cost_ext, slope_ext, grad_ref, taps_fwd, taps_bwd,
    slab, src_acc, own_acc, uses_ref, line_in, summed, paired, dense, blocks, ring_in, result, ordered,
    w_sem, ring_send, ring_recv, pair_send, pair_recv, line_send, line_recv, cost_send, cost_recv, slope_send, slope_recv,
    use_send, use_recv, both_send, both_recv, back_send, back_recv, last_send, last_recv,
):
    views, per_view, planes, pixels, n_view, n_plane, group = dims
    v, p = lax.axis_index("view"), lax.axis_index("plane")
    core = lax.rem(v, 2)
    chip = v // 2
    sibling = v + 1 - 2 * core
    chips = n_view // 2
    rows = per_view * C
    chunk = rows + C
    uses = per_view + 1
    lines = tuple(range(1, n_plane))

    def lanes(q):
        return pl.ds(pl.multiple_of(q * LANES, LANES), LANES)

    def remote(src, dst, send, recv, device):
        return pltpu.make_async_remote_copy(
            src_ref=src, dst_ref=dst, send_sem=send, recv_sem=recv, device_id=device, device_id_type=MESH)

    def along(j):
        return lax.rem(p + j, n_plane)

    weights = pltpu.make_async_copy(w_hbm, w_ref, w_sem)
    weights.start()

    into = lax.broadcasted_iota(jnp.int32, (C, C), 0)
    outof = lax.broadcasted_iota(jnp.int32, (C, C), 1)
    swap = (outof == (into % G) * GC + into // G).astype(bf16)
    for i in range(views):
        refs_ref[i] = jnp.dot(swap, feat_ref[i], preferred_element_type=f32).astype(bf16)
    quarter[pl.ds(v * views, views)] = refs_ref[:, :, lanes(p)]

    peers = [(lax.rem(v + 2 * j, n_view), p) for j in range(1, chips)]
    peers += [(sibling, p)]
    peers += [(v, along(j)) for j in lines]
    greet(peers)

    def ring_copy(j, owner, target):
        block = quarter.at[pl.ds(owner * views, views)]
        return remote(block, block, ring_send.at[j], ring_recv.at[j], (target, p))

    def pair_copy(j, owner):
        block = quarter.at[pl.ds(owner * views, views)]
        return remote(block, block, pair_send.at[j], pair_recv.at[j], (sibling, p))

    @pl.loop(1, chips)
    def _(j):
        ring_copy(j, v, lax.rem(v + 2 * j, n_view)).start()

    pair_copy(0, v).start()

    for k in range(3):
        taps = taps_ref[k]
        for g in range(G):
            taps_fwd[k * G + g] = jnp.broadcast_to(taps[:, g : g + 1], (G, LANES))
            taps_bwd[k * G + g] = jnp.broadcast_to(column(taps[g : g + 1, :]), (G, LANES))

    @pl.loop(1, chips)
    def _(j):
        owner = lax.rem(v - 2 * j + n_view, n_view)
        ring_copy(j, owner, owner).wait_recv()
        pair_copy(j, owner).start()

    @pl.loop(0, chips)
    def _(j):
        pair_copy(j, lax.rem(sibling - 2 * j + n_view, n_view)).wait_recv()

    def line_copy(r, j, q, device):
        block = tiles_ref.at[pl.ds(pl.multiple_of(r * rows, rows), rows), lanes(q)]
        return remote(block, block, line_send.at[r, j - 1], line_recv.at[r, j - 1], (v, device))

    for r in range(views):

        @pl.loop(0, per_view)
        def _(s):
            source = sources_ref[v * views + r, s]
            start = pl.multiple_of((r * per_view + s) * C, C)
            tiles_ref[pl.ds(start, C), lanes(p)] = quarter[source]

        if r > 0:
            for j in lines:
                line_copy(r - 1, j, p, along(j)).start()

    @pl.loop(1, chips)
    def _(j):
        ring_copy(j, v, lax.rem(v + 2 * j, n_view)).wait_send()

    for j in lines:
        line_copy(views - 1, j, p, along(j)).start()

    def edges(buffer, r, send, recv):
        return (
            remote(buffer.at[1, r], buffer.at[planes + 1, r], send.at[r, 0], recv.at[r, 0], (v, along(n_plane - 1))),
            remote(buffer.at[planes, r], buffer.at[0, r], send.at[r, 1], recv.at[r, 1], (v, along(1))),
        )

    def send_edges(buffer, r, send, recv):
        for copy in edges(buffer, r, send, recv):
            copy.start()

    gate_col = column(gate_ref[...])

    def forward(r, d):
        gate_b = jnp.broadcast_to(gate_col * 0.125, (G, pixels))
        warped = lax.dot_general(
            tiles_ref[pl.ds(pl.multiple_of(r * rows, rows), rows), :],
            w_ref[d],
            (((1,), (1,)), ((), ())),
            preferred_element_type=f32,
        )
        warped_ref[r, d] = warped.astype(bf16)
        ref_map = refs_ref[r].astype(f32)
        weighted = None
        for s in range(per_view):
            product = warped[s * C : (s + 1) * C] * ref_map
            corr = (product[0:8] + product[8:16]) + (product[16:24] + product[24:32])
            corr_ref[r, d, s * G : (s + 1) * G, :] = corr
            half = jnp.sum(corr * gate_b, axis=0, keepdims=True)
            turn = jnp.tanh(half)
            aux_ref[r, d, s : s + 1, :] = turn
            visible = 1.0 + 0.5 * turn
            if weighted is None:
                weighted = visible * corr
                total = visible
            else:
                weighted = weighted + visible * corr
                total = total + visible
        inverse = 1.0 / total
        aux_ref[r, d, per_view : per_view + 1, :] = inverse
        cost_ext[d + 1, r] = weighted * (inverse * 0.25)

    weights.wait()

    @pl.loop(0, views)
    def _(r):
        for j in lines:
            other = along(n_plane - j)
            line_copy(r, j, other, other).wait_recv()

        @pl.loop(0, planes // group)
        def _(step):
            for u in range(group):
                forward(r, step * group + u)

            @pl.when((step == 0) & (r > 0))
            def _():
                send_edges(cost_ext, r - 1, cost_send, cost_recv)

    def conv(buffer, taps, r, d, flip):
        total = [None] * (pixels // LANES)
        for k in range(3):
            at = d + (2 - k if flip else k)
            for g in range(G):
                tap = taps[k * G + g]
                for t in range(pixels // LANES):
                    row = buffer[at, r, g : g + 1, t * LANES : (t + 1) * LANES]
                    term = tap * jnp.broadcast_to(row, (G, LANES))
                    total[t] = term if total[t] is None else total[t] + term
        return jnp.concatenate(total, axis=1)

    def edges_in(buffer, r, send, recv):
        for copy in edges(buffer, r, send, recv):
            copy.wait()
        buffer[0, r] = buffer[0, r] * jnp.where(p == 0, 0.0, 1.0)
        buffer[planes + 1, r] = buffer[planes + 1, r] * jnp.where(p == n_plane - 1, 0.0, 1.0)

    @pl.loop(0, views)
    def _(r):
        edges_in(cost_ext, r, cost_send, cost_recv)

        @pl.loop(0, planes)
        def _(d):
            pre = conv(cost_ext, taps_fwd, r, d, False)
            gate = jax.nn.sigmoid(pre)
            regular_ref[r, d] = (pre * gate).astype(bf16)
            slope_ext[d + 1, r] = cot_ref[r, d].astype(f32) * (gate * (1.0 + pre * (1.0 - gate)))

        @pl.when(r == 0)
        def _():
            send_edges(cost_ext, views - 1, cost_send, cost_recv)

        @pl.when(r > 0)
        def _():
            send_edges(slope_ext, r - 1, slope_send, slope_recv)

    def backward(r, d, u):
        gate_b = jnp.broadcast_to(gate_col * 0.0625, (G, pixels))
        ref_map = refs_ref[r].astype(f32)
        inverse = aux_ref[r, d, per_view : per_view + 1, :]
        d_num = grad_ref[d] * (inverse * 0.25)
        cost4 = cost_ext[d + 1, r] * 4.0
        own = None
        for s in range(per_view):
            corr = corr_ref[r, d, s * G : (s + 1) * G, :]
            turn = aux_ref[r, d, s : s + 1, :]
            push = jnp.sum(d_num * (corr - cost4), axis=0, keepdims=True)
            push = push * (1.0 - turn * turn)
            d_corr = d_num * (1.0 + 0.5 * turn) + gate_b * push
            d_tile = jnp.concatenate([d_corr] * GC, axis=0)
            slab[u, s * C : (s + 1) * C, :] = (d_tile * ref_map).astype(bf16)
            part = d_tile * warped_ref[r, d, s * C : (s + 1) * C, :].astype(f32)
            own = part if own is None else own + part
        own_acc[...] += own
        src_acc[...] += jnp.dot(slab[u], w_ref[d], preferred_element_type=f32)

    def use_copy(r, j):
        part = pl.ds(pl.multiple_of(r * chunk, chunk), chunk)
        return remote(
            uses_ref.at[part, lanes(along(j))], line_in.at[j - 1, part], use_send.at[r, j - 1], use_recv.at[r, j - 1],
            (v, along(j)))

    @pl.loop(0, views)
    def _(r):
        edges_in(slope_ext, r, slope_send, slope_recv)

        @pl.loop(0, planes)
        def _(d):
            grad_ref[d] = conv(slope_ext, taps_bwd, r, d, True)

        @pl.when(r == 0)
        def _():
            send_edges(slope_ext, views - 1, slope_send, slope_recv)

        src_acc[...] = jnp.zeros_like(src_acc)
        own_acc[...] = jnp.zeros_like(own_acc)

        @pl.loop(0, planes // group)
        def _(step):
            for u in range(group):
                backward(r, step * group + u, u)

            @pl.when((step == 0) & (r > 0))
            def _():
                for j in lines:
                    use_copy(r - 1, j).start()

        uses_ref[pl.ds(pl.multiple_of(r * chunk, chunk), rows)] = src_acc[...].astype(bf16)
        uses_ref[pl.ds(pl.multiple_of(r * chunk + rows, C), C)] = own_acc[...].astype(bf16)

    place = lax.broadcasted_iota(jnp.int32, (1, LANES), 1)
    named = jnp.full((1, LANES), -1, jnp.int32)
    for half, device in enumerate((v, sibling)):
        for r in range(views):
            for s in range(per_view):
                named = jnp.where(place == half * 64 + r * uses + s, sources_ref[device * views + r, s], named)
            named = jnp.where(place == half * 64 + r * uses + per_view, device * views + r, named)
    row = lax.broadcasted_iota(jnp.int32, (chips * views, LANES), 0)
    goal = (row // views) * (2 * views) + core * views + row % views
    pick = (goal == jnp.broadcast_to(named, (chips * views, LANES))).astype(bf16)

    for j in lines:
        use_copy(views - 1, j).start()

    def both_copy(r):
        part = pl.ds(pl.multiple_of(r * chunk, chunk), chunk)
        return remote(summed.at[part], paired.at[part], both_send.at[r], both_recv.at[r], (sibling, p))

    @pl.loop(0, views)
    def _(r):
        for j in lines:
            use_copy(r, j).wait()
        part = pl.ds(pl.multiple_of(r * chunk, chunk), chunk)
        own = uses_ref[part, lanes(p)].astype(f32)
        summed[part] = own + (
            (line_in[0, part].astype(f32) + line_in[1, part].astype(f32)) + line_in[2, part].astype(f32))

        @pl.when(r > 0)
        def _():
            both_copy(r - 1).start()

    for r in range(views):
        for j in lines:
            line_copy(r, j, p, along(j)).wait_send()

    @pl.loop(0, chips)
    def _(j):
        pair_copy(j, lax.rem(v - 2 * j + n_view, n_view)).wait_send()

    both_copy(views - 1).start()
    for r in range(views):
        both_copy(r).wait()

    count = views * uses
    gap = jnp.zeros((64 - count, LANES), f32)

    @pl.loop(0, C)
    def _(c):
        stack = jnp.concatenate(
            [summed[pl.ds(c, count, stride=C), :], gap, paired[pl.ds(c, count, stride=C), :], gap], axis=0)
        high = stack.astype(bf16)
        low = (stack - high.astype(f32)).astype(bf16)
        dense[pl.ds(c, chips * views, stride=C), :] = jnp.dot(pick, high, preferred_element_type=f32) + jnp.dot(
            pick, low, preferred_element_type=f32)

    block = views * C

    def back_copy(j, target, origin):
        return remote(
            blocks.at[target], ring_in.at[origin], back_send.at[j], back_recv.at[j], (2 * target + core, p))

    def shift(j):
        return lax.rem(chip + j, chips)

    @pl.loop(1, chips)
    def _(j):
        start = pl.multiple_of(shift(j) * block, block)
        blocks[shift(j)] = dense[pl.ds(start, block), :].astype(bf16)

        @pl.when(j > 1)
        def _():
            back_copy(j - 1, shift(j - 1), chip).start()

    result[...] = dense[pl.ds(pl.multiple_of(chip * block, block), block), :]
    back_copy(chips - 1, shift(chips - 1), chip).start()

    @pl.loop(1, chips)
    def _(j):
        origin = lax.rem(chip - j + chips, chips)
        back_copy(j, chip, origin).wait_recv()
        result[...] += ring_in[origin].astype(f32)

    for i in range(views):
        for k in range(GC):
            ordered[pl.ds(i * C + k, G, stride=GC), :] = result[i * C + k * G : i * C + (k + 1) * G, :]
        out_ref[i, :, lanes(p)] = ordered[i * C : (i + 1) * C, :]

    @pl.loop(1, chips)
    def _(j):
        back_copy(j, shift(j), chip).wait_send()

    def last_copy(j, q, target):
        part = out_ref.at[:, :, lanes(q)]
        return remote(part, part, last_send.at[j - 1], last_recv.at[j - 1], (v, target))

    for j in lines:
        last_copy(j, p, along(j)).start()
    for j in lines:
        other = along(n_plane - j)
        last_copy(j, p, along(j)).wait_send()
        last_copy(j, other, other).wait_recv()


def shards(n_view, n_plane, features, sources, warp_weights, view_gate, depth_kernel, cotangent):
    views, channels, pixels = features.shape
    per_view = sources.shape[1]
    planes = warp_weights.shape[0]
    chips = n_view // 2
    rows = per_view * channels
    chunk = rows + channels
    group = 4
    lines = n_plane - 1
    dma = pltpu.SemaphoreType.DMA
    vmem = pl.BlockSpec(memory_space=pltpu.VMEM)
    return pl.pallas_call(
        functools.partial(sweep_kernel, (views, per_view, planes, pixels, n_view, n_plane, group)),
        in_specs=[vmem, pl.BlockSpec(memory_space=pltpu.SMEM), pl.BlockSpec(memory_space=pl.ANY), vmem, vmem, vmem],
        out_specs=[vmem, vmem],
        out_shape=[
            jax.ShapeDtypeStruct(cotangent.shape, bf16),
            jax.ShapeDtypeStruct(features.shape, f32),
        ],
        scratch_shapes=[
            pltpu.VMEM(warp_weights.shape, bf16),
            pltpu.VMEM(features.shape, bf16),
            pltpu.VMEM((n_view * views, channels, LANES), bf16),
            pltpu.VMEM((views * rows, pixels), bf16),
            pltpu.VMEM((views, planes, rows, pixels), bf16),
            pltpu.VMEM((views, planes, per_view * G, pixels), f32),
            pltpu.VMEM((views, planes, 16, pixels), f32),
            pltpu.VMEM((planes + 2, views, G, pixels), f32),
            pltpu.VMEM((planes + 2, views, G, pixels), f32),
            pltpu.VMEM((planes, G, pixels), f32),
            pltpu.VMEM((3 * G, G, LANES), f32),
            pltpu.VMEM((3 * G, G, LANES), f32),
            pltpu.VMEM((group, rows, pixels), bf16),
            pltpu.VMEM((rows, pixels), f32),
            pltpu.VMEM((channels, pixels), f32),
            pltpu.VMEM((views * chunk, pixels), bf16),
            pltpu.VMEM((lines, views * chunk, LANES), bf16),
            pltpu.VMEM((views * chunk, LANES), f32),
            pltpu.VMEM((views * chunk, LANES), f32),
            pltpu.VMEM((chips * views * channels, LANES), f32),
            pltpu.VMEM((chips, views * channels, LANES), bf16),
            pltpu.VMEM((chips, views * channels, LANES), bf16),
            pltpu.VMEM((views * channels, LANES), f32),
            pltpu.VMEM((views * channels, LANES), f32),
            dma,
            dma((chips,)), dma((chips,)), dma((chips,)), dma((chips,)),
            dma((views, lines)), dma((views, lines)),
            dma((views, 2)), dma((views, 2)), dma((views, 2)), dma((views, 2)),
            dma((views, lines)), dma((views, lines)),
            dma((views,)), dma((views,)),
            dma((chips,)), dma((chips,)),
            dma((lines,)), dma((lines,)),
        ],
        compiler_params=pltpu.CompilerParams(collective_id=0, has_side_effects=True),
        name="plane_sweep",
    )(features, sources, warp_weights, view_gate.reshape(1, G), depth_kernel, cotangent)


def solution(mesh):
    in_specs = (
        P("view", None, None),
        P(),
        P("plane", None, None),
        P(),
        P(),
        P("view", "plane", None, None),
    )
    out_specs = (P("view", "plane", None, None), P("view", None, None))
    body = functools.partial(shards, mesh.shape["view"], mesh.shape["plane"])
    return jax.shard_map(body, mesh=mesh, in_specs=in_specs, out_specs=out_specs, check_vma=False)
```

```python
import functools

import jax
import jax.numpy as jnp
from jax import lax
from jax.experimental import pallas as pl
from jax.experimental.pallas import tpu as pltpu
from jax.sharding import PartitionSpec as P

G = 8
GC = 4
C = G * GC
LANES = 128
MESH = pl.DeviceIdType.MESH
f32 = jnp.float32
bf16 = jnp.bfloat16


def column(row):
    eye = lax.broadcasted_iota(jnp.int32, (G, G), 0) == lax.broadcasted_iota(jnp.int32, (G, G), 1)
    return jnp.sum(jnp.where(eye, jnp.broadcast_to(row, (G, G)), 0.0), axis=1, keepdims=True)


def greet(peers):
    barrier = pltpu.get_barrier_semaphore()
    for peer in peers:
        pl.semaphore_signal(barrier, inc=1, device_id=peer, device_id_type=MESH)
    pl.semaphore_wait(barrier, len(peers))


def sweep_kernel(
    dims,
    feat_ref, sources_ref, w_hbm, gate_ref, taps_ref, cot_ref,
    regular_ref, out_ref,
    w_ref, refs_ref, pool, select, tiles_ref, warped_ref, corr_ref, aux_ref, cost_ext, slope_ext, grad_ref, taps_fwd, taps_bwd,
    slab, src_acc, own_acc, uses_ref, relay_in, merged, side_in, mate_in, summed, dense, blocks, ring_in, result, final_in, ordered,
    w_sem, ring_send, ring_recv, line_send, line_recv, mate_send, mate_recv, pass_send,
    cost_send, cost_recv, slope_send, slope_recv,
    first_send, first_recv, side_send, side_recv, match_send, match_recv, back_send, back_recv, last_send, last_recv,
):
    views, per_view, planes, pixels, n_view, n_plane, group = dims
    v, p = lax.axis_index("view"), lax.axis_index("plane")
    core = lax.rem(v, 2)
    chip = v // 2
    sibling = v + 1 - 2 * core
    chips = n_view // 2
    half = C // 2
    rows = per_view * half
    uses = per_view + 1
    full = uses * half

    def lanes(q):
        return pl.ds(pl.multiple_of(q * LANES, LANES), LANES)

    def remote(src, dst, send, recv, device):
        return pltpu.make_async_remote_copy(
            src_ref=src, dst_ref=dst, send_sem=send, recv_sem=recv, device_id=device, device_id_type=MESH)

    def along(j):
        return lax.rem(p + j + n_plane, n_plane)

    weights = pltpu.make_async_copy(w_hbm, w_ref, w_sem)
    weights.start()

    into = lax.broadcasted_iota(jnp.int32, (C, C), 0)
    outof = lax.broadcasted_iota(jnp.int32, (C, C), 1)
    swap = (outof == (into % G) * GC + into // G).astype(bf16)
    for i in range(views):
        refs_ref[i] = jnp.dot(swap, feat_ref[i], preferred_element_type=f32).astype(bf16)
    pool[pl.ds(v * views, views)] = refs_ref[:, pl.ds(pl.multiple_of(core * half, half), half), lanes(p)]

    peers = [(lax.rem(v + j, n_view), p) for j in range(1, n_view)]
    peers += [(2 * chip + c, along(j)) for c in range(2) for j in range(1, n_plane)]
    greet(peers)

    def ring_copy(j):
        target = lax.rem(v + j, n_view)
        part = refs_ref.at[:, pl.ds(pl.multiple_of(lax.rem(target, 2) * half, half), half), lanes(p)]
        return remote(part, pool.at[pl.ds(v * views, views)], ring_send.at[j], ring_recv.at[j], (target, p))

    def ring_arrived(j):
        owner = lax.rem(v - j + n_view, n_view)
        part = pool.at[pl.ds(owner * views, views)]
        return remote(part, part, ring_send.at[j], ring_recv.at[j], (owner, p))

    @pl.loop(1, n_view)
    def _(j):
        ring_copy(j).start()

    for k in range(3):
        taps = taps_ref[k]
        for g in range(G):
            taps_fwd[k * G + g] = jnp.broadcast_to(taps[:, g : g + 1], (G, LANES))
            taps_bwd[k * G + g] = jnp.broadcast_to(column(taps[g : g + 1, :]), (G, LANES))

    @pl.loop(1, n_view)
    def _(j):
        ring_arrived(j).wait_recv()

    def line_copies(r):
        copies = []
        for step in (1, -1):
            for c in range(2):
                slot = 0 if step == 1 else 1
                copies.append(
                    remote(
                        select.at[c, r], tiles_ref.at[r, core, :, lanes(p)], line_send.at[r, slot, c],
                        line_recv.at[r, slot, core], (2 * chip + c, along(step))))
        copies.append(
            remote(
                select.at[1 - core, r], tiles_ref.at[r, core, :, lanes(p)], mate_send.at[r], mate_recv.at[r],
                (sibling, p)))
        return copies

    onward = 1 - 2 * core

    def pass_copies(r):
        return [
            remote(
                tiles_ref.at[r, h, :, lanes(along(-onward))], tiles_ref.at[r, h, :, lanes(along(-onward))],
                pass_send.at[r, h], line_recv.at[r, 2, h], (v, along(onward)))
            for h in range(2)
        ]

    def line_arrived(r, slot, h, q):
        part = tiles_ref.at[r, h, :, lanes(q)]
        return remote(part, part, pass_send.at[r, h], line_recv.at[r, slot, h], (v, q))

    def relay_maps(r):
        for h in range(2):
            line_arrived(r, core, h, along(-onward)).wait_recv()
        for copy in pass_copies(r):
            copy.start()

    def maps_arrived(r):
        for h in range(2):
            line_arrived(r, 1 - core, h, along(onward)).wait_recv()
            line_arrived(r, 2, h, along(2)).wait_recv()
        part = tiles_ref.at[r, 1 - core, :, lanes(p)]
        remote(part, part, mate_send.at[r], mate_recv.at[r], (sibling, p)).wait_recv()

    for r in range(views):

        @pl.loop(0, per_view)
        def _(s):
            start = pl.multiple_of(s * half, half)
            for c in range(2):
                select[c, r, pl.ds(start, half)] = pool[sources_ref[(2 * chip + c) * views + r, s]]
            tiles_ref[r, core, pl.ds(start, half), lanes(p)] = pool[sources_ref[v * views + r, s]]

        if r > 0:
            for copy in line_copies(r - 1):
                copy.start()

    @pl.loop(1, n_view)
    def _(j):
        ring_copy(j).wait_send()

    for copy in line_copies(views - 1):
        copy.start()
    relay_maps(0)

    def edges(buffer, r, send, recv):
        return (
            remote(buffer.at[1, r], buffer.at[planes + 1, r], send.at[r, 0], recv.at[r, 0], (v, along(-1))),
            remote(buffer.at[planes, r], buffer.at[0, r], send.at[r, 1], recv.at[r, 1], (v, along(1))),
        )

    def send_edges(buffer, r, send, recv):
        for copy in edges(buffer, r, send, recv):
            copy.start()

    gate_col = column(gate_ref[...])

    def pieces(maps, s):
        at = s * half
        return maps[at : at + G], maps[at + G : at + half], maps[rows + at : rows + at + G], maps[rows + at + G : rows + at + half]

    def forward(r, d):
        gate_b = jnp.broadcast_to(gate_col * 0.125, (G, pixels))
        warped = lax.dot_general(
            tiles_ref[r].reshape(2 * rows, pixels),
            w_ref[d],
            (((1,), (1,)), ((), ())),
            preferred_element_type=f32,
        )
        warped_ref[r, d] = warped.astype(bf16)
        ref_map = refs_ref[r].astype(f32)
        refs = [ref_map[k * G : (k + 1) * G] for k in range(GC)]
        weighted = None
        for s in range(per_view):
            terms = [one * ref for one, ref in zip(pieces(warped, s), refs)]
            corr = (terms[0] + terms[1]) + (terms[2] + terms[3])
            corr_ref[r, d, s * G : (s + 1) * G, :] = corr
            logit = jnp.sum(corr * gate_b, axis=0, keepdims=True)
            turn = jnp.tanh(logit)
            aux_ref[r, d, s : s + 1, :] = turn
            visible = 1.0 + 0.5 * turn
            if weighted is None:
                weighted = visible * corr
                total = visible
            else:
                weighted = weighted + visible * corr
                total = total + visible
        inverse = 1.0 / total
        aux_ref[r, d, per_view : per_view + 1, :] = inverse
        cost_ext[d + 1, r] = weighted * (inverse * 0.25)

    weights.wait()

    @pl.loop(0, views)
    def _(r):
        maps_arrived(r)

        @pl.loop(0, planes // group)
        def _(step):
            for u in range(group):
                forward(r, step * group + u)

            @pl.when((step == 0) & (r < views - 1))
            def _():
                relay_maps(r + 1)

            @pl.when((step == 0) & (r > 0))
            def _():
                send_edges(cost_ext, r - 1, cost_send, cost_recv)

    def conv(buffer, taps, r, d, flip):
        total = [None] * (pixels // LANES)
        for k in range(3):
            at = d + (2 - k if flip else k)
            for g in range(G):
                tap = taps[k * G + g]
                for t in range(pixels // LANES):
                    row = buffer[at, r, g : g + 1, t * LANES : (t + 1) * LANES]
                    term = tap * jnp.broadcast_to(row, (G, LANES))
                    total[t] = term if total[t] is None else total[t] + term
        return jnp.concatenate(total, axis=1)

    def edges_in(buffer, r, send, recv):
        for copy in edges(buffer, r, send, recv):
            copy.wait()
        buffer[0, r] = buffer[0, r] * jnp.where(p == 0, 0.0, 1.0)
        buffer[planes + 1, r] = buffer[planes + 1, r] * jnp.where(p == n_plane - 1, 0.0, 1.0)

    @pl.loop(0, views)
    def _(r):
        edges_in(cost_ext, r, cost_send, cost_recv)

        @pl.loop(0, planes)
        def _(d):
            pre = conv(cost_ext, taps_fwd, r, d, False)
            gate = jax.nn.sigmoid(pre)
            regular_ref[r, d] = (pre * gate).astype(bf16)
            slope_ext[d + 1, r] = cot_ref[r, d].astype(f32) * (gate * (1.0 + pre * (1.0 - gate)))

        @pl.when(r == 0)
        def _():
            send_edges(cost_ext, views - 1, cost_send, cost_recv)

        @pl.when(r > 0)
        def _():
            send_edges(slope_ext, r - 1, slope_send, slope_recv)

    def backward(r, d, u):
        gate_b = jnp.broadcast_to(gate_col * 0.0625, (G, pixels))
        ref_map = refs_ref[r].astype(f32)
        refs = [ref_map[k * G : (k + 1) * G] for k in range(GC)]
        inverse = aux_ref[r, d, per_view : per_view + 1, :]
        d_num = grad_ref[d] * (inverse * 0.25)
        cost4 = cost_ext[d + 1, r] * 4.0
        own = [None] * GC
        for s in range(per_view):
            corr = corr_ref[r, d, s * G : (s + 1) * G, :]
            turn = aux_ref[r, d, s : s + 1, :]
            push = jnp.sum(d_num * (corr - cost4), axis=0, keepdims=True)
            push = push * (1.0 - turn * turn)
            d_corr = d_num * (1.0 + 0.5 * turn) + gate_b * push
            for h in range(2):
                at = pl.ds(h * rows + s * half, half)
                slab[u, at, :] = jnp.concatenate([d_corr * refs[2 * h], d_corr * refs[2 * h + 1]], axis=0).astype(bf16)
                saved = warped_ref[r, d, at, :].astype(f32)
                for k in range(2):
                    part = d_corr * saved[k * G : (k + 1) * G]
                    own[2 * h + k] = part if own[2 * h + k] is None else own[2 * h + k] + part
        own_acc[...] += jnp.concatenate(own, axis=0)
        src_acc[...] += jnp.dot(slab[u], w_ref[d], preferred_element_type=f32)

    def first_copies(r):
        return [
            remote(
                uses_ref.at[h, r, :, lanes(along(2))], relay_in.at[h, r], first_send.at[r, h], first_recv.at[r, h],
                (v, along(1 - 2 * h)))
            for h in range(2)
        ]

    def plain_copies(r):
        copies = []
        for h in range(2):
            copies.append(
                remote(
                    uses_ref.at[h, r, :, lanes(along(2 * h - 1))], side_in.at[core, 1 - h, r], side_send.at[r, h, 0],
                    side_recv.at[r, core, 1 - h], (2 * chip + h, along(2 * h - 1))))
        copies.append(
            remote(
                uses_ref.at[1 - core, r, :, lanes(p)], mate_in.at[r], match_send.at[r], match_recv.at[r], (sibling, p)))
        return copies

    def merged_copies(r):
        return [
            remote(
                merged.at[h, r], side_in.at[core, h, r], side_send.at[r, h, 1], side_recv.at[r, core, h],
                (2 * chip + h, along(1 - 2 * h)))
            for h in range(2)
        ]

    def send_uses(r):
        for copy in first_copies(r) + plain_copies(r):
            copy.start()

    def merge(r):
        for h, copy in enumerate(first_copies(r)):
            copy.wait_recv()
            own = uses_ref[h, r, :, lanes(along(1 - 2 * h))].astype(f32)
            merged[h, r] = (own + relay_in[h, r].astype(f32)).astype(bf16)

    def send_merged(r):
        for copy in merged_copies(r):
            copy.start()

    @pl.loop(0, views)
    def _(r):
        edges_in(slope_ext, r, slope_send, slope_recv)

        @pl.loop(0, planes)
        def _(d):
            grad_ref[d] = conv(slope_ext, taps_bwd, r, d, True)

        @pl.when(r == 0)
        def _():
            send_edges(slope_ext, views - 1, slope_send, slope_recv)

        src_acc[...] = jnp.zeros_like(src_acc)
        own_acc[...] = jnp.zeros_like(own_acc)

        @pl.loop(0, planes // group)
        def _(step):
            for u in range(group):
                backward(r, step * group + u, u)

            @pl.when((step == 0) & (r > 0))
            def _():
                send_uses(r - 1)

            @pl.when((step == 0) & (r > 1))
            def _():
                send_merged(r - 2)

            @pl.when((step == planes // group - 1) & (r > 0))
            def _():
                merge(r - 1)

        for h in range(2):
            uses_ref[h, r, 0:rows] = src_acc[h * rows : (h + 1) * rows].astype(bf16)
            uses_ref[h, r, rows:full] = own_acc[h * half : (h + 1) * half].astype(bf16)

    place = lax.broadcasted_iota(jnp.int32, (1, LANES), 1)
    named = jnp.full((1, LANES), -1, jnp.int32)
    for c in range(2):
        for r in range(views):
            first = (2 * chip + c) * views + r
            for s in range(per_view):
                named = jnp.where(place == c * 64 + r * uses + s, sources_ref[first, s], named)
            named = jnp.where(place == c * 64 + r * uses + per_view, first, named)
    count = views * uses
    owned = chips * views
    row = lax.broadcasted_iota(jnp.int32, (2 * owned, 2 * LANES), 0)
    goal = ((row % owned) // views) * (2 * views) + (row // owned) * views + row % views
    pick = (goal == jnp.concatenate([named, named], axis=1)).astype(bf16)

    send_uses(views - 1)
    send_merged(views - 2)
    merge(views - 1)

    def side_arrived(r, c, side):
        part = side_in.at[c, side, r]
        return remote(part, part, side_send.at[r, 0, 0], side_recv.at[r, c, side], (v, p))

    def total(r):
        for c in range(2):
            for side in range(2):
                side_arrived(r, c, side).wait_recv()
        remote(mate_in.at[r], mate_in.at[r], match_send.at[r], match_recv.at[r], (sibling, p)).wait_recv()
        mine = uses_ref[core, r, :, lanes(p)].astype(f32)
        for c in range(2):
            here = jnp.where(core == c, mine, mate_in[r].astype(f32))
            start = pl.multiple_of((c * views + r) * full, half)
            summed[pl.ds(start, full)] = here + (side_in[c, 0, r].astype(f32) + side_in[c, 1, r].astype(f32))

    total(0)
    send_merged(views - 1)

    @pl.loop(1, views)
    def _(r):
        total(r)

    gap = jnp.zeros((64 - count, LANES), f32)
    for at in range(half):
        stack = jnp.concatenate(
            [
                summed[pl.ds(at, count, stride=half), :], gap,
                summed[pl.ds(views * full + at, count, stride=half), :], gap,
            ],
            axis=0)
        high = stack.astype(bf16)
        low = (stack - high.astype(f32)).astype(bf16)
        dense[pl.ds(at, 2 * owned, stride=half), :] = jnp.dot(
            pick, jnp.concatenate([high, low], axis=0), preferred_element_type=f32)

    block = views * half

    def shift(j):
        return lax.rem(chip + j, chips)

    def back_copy(a, j):
        return remote(
            blocks.at[a, shift(j)], ring_in.at[a, chip], back_send.at[a, j], back_recv.at[a, j],
            (2 * shift(j) + core, p))

    for a in range(2):

        @pl.loop(1, chips)
        def _(j):
            start = pl.multiple_of((a * chips + shift(j)) * block, block)
            blocks[a, shift(j)] = dense[pl.ds(start, block), :].astype(bf16)

            @pl.when(j > 1)
            def _():
                back_copy(a, j - 1).start()

        result[a] = dense[pl.ds(pl.multiple_of((a * chips + chip) * block, block), block), :]
        back_copy(a, chips - 1).start()

    def last_copies(a):
        return [
            remote(
                result.at[a], final_in.at[p, core], last_send.at[a, j], last_recv.at[j, core],
                (2 * chip + a, along(j)))
            for j in range(1, n_plane)
        ]

    def mate_copy():
        return remote(
            result.at[1 - core], final_in.at[p, core], last_send.at[1 - core, 0], last_recv.at[0, core], (sibling, p))

    for a in range(2):

        @pl.loop(1, chips)
        def _(j):
            origin = lax.rem(chip - j + chips, chips)
            part = ring_in.at[a, origin]
            remote(part, part, back_send.at[a, j], back_recv.at[a, j], (v, p)).wait_recv()
            result[a] += ring_in[a, origin].astype(f32)

        if a == 0:

            @pl.loop(1, chips)
            def _(j):
                back_copy(0, j).wait_send()

            for copy in last_copies(0):
                copy.start()

    final_in[p, core] = result[core]

    @pl.loop(1, chips)
    def _(j):
        back_copy(1, j).wait_send()

    for copy in last_copies(1):
        copy.start()
    mate_copy().start()

    for r in range(views):
        for copy in line_copies(r) + pass_copies(r) + first_copies(r) + plain_copies(r) + merged_copies(r):
            copy.wait_send()

    def reorder(q):
        for h in range(2):
            for i in range(views):
                for k in range(2):
                    ordered[q, pl.ds(i * C + 2 * h + k, G, stride=GC), :] = final_in[q, h, pl.ds(i * half + k * G, G), :]
        for i in range(views):
            out_ref[i, :, lanes(q)] = ordered[q, i * C : (i + 1) * C, :]

    def last_arrived(j, h):
        q = along(-j)
        part = final_in.at[q, h]
        return remote(part, part, last_send.at[0, j], last_recv.at[j, h], (v, q))

    last_arrived(0, 1 - core).wait_recv()
    reorder(p)
    for j in (1, 3, 2):
        for h in range(2):
            last_arrived(j, h).wait_recv()
        reorder(along(-j))
    for a in range(2):
        for copy in last_copies(a):
            copy.wait_send()
    mate_copy().wait_send()


def shards(n_view, n_plane, features, sources, warp_weights, view_gate, depth_kernel, cotangent):
    views, channels, pixels = features.shape
    per_view = sources.shape[1]
    planes = warp_weights.shape[0]
    chips = n_view // 2
    half = channels // 2
    rows = per_view * half
    full = rows + half
    group = 4
    dma = pltpu.SemaphoreType.DMA
    vmem = pl.BlockSpec(memory_space=pltpu.VMEM)
    return pl.pallas_call(
        functools.partial(sweep_kernel, (views, per_view, planes, pixels, n_view, n_plane, group)),
        in_specs=[vmem, pl.BlockSpec(memory_space=pltpu.SMEM), pl.BlockSpec(memory_space=pl.ANY), vmem, vmem, vmem],
        out_specs=[vmem, vmem],
        out_shape=[
            jax.ShapeDtypeStruct(cotangent.shape, bf16),
            jax.ShapeDtypeStruct(features.shape, f32),
        ],
        scratch_shapes=[
            pltpu.VMEM(warp_weights.shape, bf16),
            pltpu.VMEM(features.shape, bf16),
            pltpu.VMEM((n_view * views, half, LANES), bf16),
            pltpu.VMEM((2, views, rows, LANES), bf16),
            pltpu.VMEM((views, 2, rows, pixels), bf16),
            pltpu.VMEM((views, planes, 2 * rows, pixels), bf16),
            pltpu.VMEM((views, planes, per_view * G, pixels), f32),
            pltpu.VMEM((views, planes, 16, pixels), f32),
            pltpu.VMEM((planes + 2, views, G, pixels), f32),
            pltpu.VMEM((planes + 2, views, G, pixels), f32),
            pltpu.VMEM((planes, G, pixels), f32),
            pltpu.VMEM((3 * G, G, LANES), f32),
            pltpu.VMEM((3 * G, G, LANES), f32),
            pltpu.VMEM((group, 2 * rows, pixels), bf16),
            pltpu.VMEM((2 * rows, pixels), f32),
            pltpu.VMEM((channels, pixels), f32),
            pltpu.VMEM((2, views, full, pixels), bf16),
            pltpu.VMEM((2, views, full, LANES), bf16),
            pltpu.VMEM((2, views, full, LANES), bf16),
            pltpu.VMEM((2, 2, views, full, LANES), bf16),
            pltpu.VMEM((views, full, LANES), bf16),
            pltpu.VMEM((2 * views * full, LANES), f32),
            pltpu.VMEM((2 * chips * views * half, LANES), f32),
            pltpu.VMEM((2, chips, views * half, LANES), bf16),
            pltpu.VMEM((2, chips, views * half, LANES), bf16),
            pltpu.VMEM((2, views * half, LANES), f32),
            pltpu.VMEM((n_plane, 2, views * half, LANES), f32),
            pltpu.VMEM((n_plane, views * channels, LANES), f32),
            dma,
            dma((n_view,)), dma((n_view,)),
            dma((views, 2, 2)), dma((views, 3, 2)), dma((views,)), dma((views,)), dma((views, 2)),
            dma((views, 2)), dma((views, 2)), dma((views, 2)), dma((views, 2)),
            dma((views, 2)), dma((views, 2)), dma((views, 2, 2)), dma((views, 2, 2)), dma((views,)), dma((views,)),
            dma((2, chips)), dma((2, chips)), dma((2, n_plane)), dma((n_plane, 2)),
        ],
        compiler_params=pltpu.CompilerParams(collective_id=0, has_side_effects=True),
        name="plane_sweep",
    )(features, sources, warp_weights, view_gate.reshape(1, G), depth_kernel, cotangent)


def solution(mesh):
    in_specs = (
        P("view", None, None),
        P(),
        P("plane", None, None),
        P(),
        P(),
        P("view", "plane", None, None),
    )
    out_specs = (P("view", "plane", None, None), P("view", None, None))
    body = functools.partial(shards, mesh.shape["view"], mesh.shape["plane"])
    return jax.shard_map(body, mesh=mesh, in_specs=in_specs, out_specs=out_specs, check_vma=False)
```

```python
import functools

import jax
import jax.numpy as jnp
from jax import lax
from jax.experimental import pallas as pl
from jax.experimental.pallas import tpu as pltpu
from jax.sharding import PartitionSpec as P

G = 8
GC = 4
C = G * GC
LANES = 128
MESH = pl.DeviceIdType.MESH
f32 = jnp.float32
bf16 = jnp.bfloat16


def column(row):
    eye = lax.broadcasted_iota(jnp.int32, (G, G), 0) == lax.broadcasted_iota(jnp.int32, (G, G), 1)
    return jnp.sum(jnp.where(eye, jnp.broadcast_to(row, (G, G)), 0.0), axis=1, keepdims=True)


def greet(peers):
    barrier = pltpu.get_barrier_semaphore()
    for peer in peers:
        pl.semaphore_signal(barrier, inc=1, device_id=peer, device_id_type=MESH)
    pl.semaphore_wait(barrier, len(peers))


def sweep_kernel(
    dims,
    feat_ref, sources_ref, w_hbm, gate_ref, taps_ref, cot_ref,
    regular_ref, out_ref,
    w_ref, refs_ref, pool, select, tiles_ref, warped_ref, corr_ref, aux_ref, cost_ext, slope_ext, grad_ref, taps_fwd, taps_bwd,
    slab, src_acc, own_acc, uses_ref, side_in, mate_in, summed, dense, blocks, ring_in, result, final_in, ordered,
    w_sem, ring_send, ring_recv, line_send, line_recv, mate_send, mate_recv,
    cost_send, cost_recv, slope_send, slope_recv,
    side_send, side_recv, match_send, match_recv, back_send, back_recv, last_send, last_recv,
):
    views, per_view, planes, pixels, n_view, n_plane, group = dims
    v, p = lax.axis_index("view"), lax.axis_index("plane")
    core = lax.rem(v, 2)
    chip = v // 2
    sibling = v + 1 - 2 * core
    chips = n_view // 2
    half = C // 2
    rows = per_view * half
    uses = per_view + 1
    full = uses * half

    def lanes(q):
        return pl.ds(pl.multiple_of(q * LANES, LANES), LANES)

    def remote(src, dst, send, recv, device):
        return pltpu.make_async_remote_copy(
            src_ref=src, dst_ref=dst, send_sem=send, recv_sem=recv, device_id=device, device_id_type=MESH)

    def along(j):
        return lax.rem(p + j + n_plane, n_plane)

    weights = pltpu.make_async_copy(w_hbm, w_ref, w_sem)
    weights.start()

    into = lax.broadcasted_iota(jnp.int32, (C, C), 0)
    outof = lax.broadcasted_iota(jnp.int32, (C, C), 1)
    swap = (outof == (into % G) * GC + into // G).astype(bf16)
    for i in range(views):
        refs_ref[i] = jnp.dot(swap, feat_ref[i], preferred_element_type=f32).astype(bf16)
    pool[pl.ds(v * views, views)] = refs_ref[:, pl.ds(pl.multiple_of(core * half, half), half), lanes(p)]

    peers = [(lax.rem(v + j, n_view), p) for j in range(1, n_view)]
    peers += [(2 * chip + c, along(j)) for c in range(2) for j in range(1, n_plane)]
    greet(peers)

    def ring_copy(j):
        target = lax.rem(v + j, n_view)
        part = refs_ref.at[:, pl.ds(pl.multiple_of(lax.rem(target, 2) * half, half), half), lanes(p)]
        return remote(part, pool.at[pl.ds(v * views, views)], ring_send.at[j], ring_recv.at[j], (target, p))

    def ring_arrived(j):
        owner = lax.rem(v - j + n_view, n_view)
        part = pool.at[pl.ds(owner * views, views)]
        return remote(part, part, ring_send.at[j], ring_recv.at[j], (owner, p))

    @pl.loop(1, n_view)
    def _(j):
        ring_copy(j).start()

    for k in range(3):
        taps = taps_ref[k]
        for g in range(G):
            taps_fwd[k * G + g] = jnp.broadcast_to(taps[:, g : g + 1], (G, LANES))
            taps_bwd[k * G + g] = jnp.broadcast_to(column(taps[g : g + 1, :]), (G, LANES))

    @pl.loop(1, n_view)
    def _(j):
        ring_arrived(j).wait_recv()

    def line_copies(r):
        copies = [
            remote(
                select.at[c, r], tiles_ref.at[r, core, :, lanes(p)], line_send.at[r, j, c], line_recv.at[r, j, core],
                (2 * chip + c, along(j)))
            for j in (2, 1, 3)
            for c in range(2)
        ]
        copies.append(
            remote(
                select.at[1 - core, r], tiles_ref.at[r, core, :, lanes(p)], mate_send.at[r], mate_recv.at[r],
                (sibling, p)))
        return copies

    def maps_arrived(r):
        for j in range(1, n_plane):
            for h in range(2):
                part = tiles_ref.at[r, h, :, lanes(along(-j))]
                remote(part, part, line_send.at[r, j, h], line_recv.at[r, j, h], (v, along(-j))).wait_recv()
        part = tiles_ref.at[r, 1 - core, :, lanes(p)]
        remote(part, part, mate_send.at[r], mate_recv.at[r], (sibling, p)).wait_recv()

    for r in range(views):

        @pl.loop(0, per_view)
        def _(s):
            start = pl.multiple_of(s * half, half)
            for c in range(2):
                select[c, r, pl.ds(start, half)] = pool[sources_ref[(2 * chip + c) * views + r, s]]
            tiles_ref[r, core, pl.ds(start, half), lanes(p)] = pool[sources_ref[v * views + r, s]]

        if r > 0:
            for copy in line_copies(r - 1):
                copy.start()

    @pl.loop(1, n_view)
    def _(j):
        ring_copy(j).wait_send()

    for copy in line_copies(views - 1):
        copy.start()

    def edges(buffer, r, send, recv):
        return (
            remote(buffer.at[1, r], buffer.at[planes + 1, r], send.at[r, 0], recv.at[r, 0], (v, along(-1))),
            remote(buffer.at[planes, r], buffer.at[0, r], send.at[r, 1], recv.at[r, 1], (v, along(1))),
        )

    def send_edges(buffer, r, send, recv):
        for copy in edges(buffer, r, send, recv):
            copy.start()

    gate_col = column(gate_ref[...])

    def pieces(maps, s):
        at = s * half
        return maps[at : at + G], maps[at + G : at + half], maps[rows + at : rows + at + G], maps[rows + at + G : rows + at + half]

    def forward(r, d):
        gate_b = jnp.broadcast_to(gate_col * 0.125, (G, pixels))
        warped = lax.dot_general(
            tiles_ref[r].reshape(2 * rows, pixels),
            w_ref[d],
            (((1,), (1,)), ((), ())),
            preferred_element_type=f32,
        )
        warped_ref[r, d] = warped.astype(bf16)
        ref_map = refs_ref[r].astype(f32)
        refs = [ref_map[k * G : (k + 1) * G] for k in range(GC)]
        weighted = None
        for s in range(per_view):
            terms = [one * ref for one, ref in zip(pieces(warped, s), refs)]
            corr = (terms[0] + terms[1]) + (terms[2] + terms[3])
            corr_ref[r, d, s * G : (s + 1) * G, :] = corr
            logit = jnp.sum(corr * gate_b, axis=0, keepdims=True)
            turn = jnp.tanh(logit)
            aux_ref[r, d, s : s + 1, :] = turn
            visible = 1.0 + 0.5 * turn
            if weighted is None:
                weighted = visible * corr
                total = visible
            else:
                weighted = weighted + visible * corr
                total = total + visible
        inverse = 1.0 / total
        aux_ref[r, d, per_view : per_view + 1, :] = inverse
        cost_ext[d + 1, r] = weighted * (inverse * 0.25)

    def conv(buffer, taps, r, d, flip):
        total = [None] * (pixels // LANES)
        for k in range(3):
            at = d + (2 - k if flip else k)
            for g in range(G):
                tap = taps[k * G + g]
                for t in range(pixels // LANES):
                    row = buffer[at, r, g : g + 1, t * LANES : (t + 1) * LANES]
                    term = tap * jnp.broadcast_to(row, (G, LANES))
                    total[t] = term if total[t] is None else total[t] + term
        return jnp.concatenate(total, axis=1)

    def edges_in(buffer, r, send, recv):
        for copy in edges(buffer, r, send, recv):
            copy.wait()
        buffer[0, r] = buffer[0, r] * jnp.where(p == 0, 0.0, 1.0)
        buffer[planes + 1, r] = buffer[planes + 1, r] * jnp.where(p == n_plane - 1, 0.0, 1.0)

    def activate(r):
        edges_in(cost_ext, r, cost_send, cost_recv)

        @pl.loop(0, planes)
        def _(d):
            pre = conv(cost_ext, taps_fwd, r, d, False)
            gate = jax.nn.sigmoid(pre)
            regular_ref[r, d] = (pre * gate).astype(bf16)
            slope_ext[d + 1, r] = cot_ref[r, d].astype(f32) * (gate * (1.0 + pre * (1.0 - gate)))

    weights.wait()

    @pl.loop(0, views)
    def _(r):
        maps_arrived(r)

        @pl.loop(0, planes // group)
        def _(step):
            for u in range(group):
                at = step * group + u
                forward(r, jnp.where(at == 0, 0, jnp.where(at == 1, planes - 1, at - 1)))

            @pl.when((step == 0) & (r > 1))
            def _():
                activate(r - 2)

            @pl.when(step == 1)
            def _():
                send_edges(cost_ext, r, cost_send, cost_recv)

            @pl.when((step == 1) & (r > 1))
            def _():
                send_edges(slope_ext, r - 2, slope_send, slope_recv)

    activate(views - 2)

    def backward(r, d, u):
        gate_b = jnp.broadcast_to(gate_col * 0.0625, (G, pixels))
        ref_map = refs_ref[r].astype(f32)
        refs = [ref_map[k * G : (k + 1) * G] for k in range(GC)]
        inverse = aux_ref[r, d, per_view : per_view + 1, :]
        d_num = grad_ref[d] * (inverse * 0.25)
        cost4 = cost_ext[d + 1, r] * 4.0
        own = [None] * GC
        for s in range(per_view):
            corr = corr_ref[r, d, s * G : (s + 1) * G, :]
            turn = aux_ref[r, d, s : s + 1, :]
            push = jnp.sum(d_num * (corr - cost4), axis=0, keepdims=True)
            push = push * (1.0 - turn * turn)
            d_corr = d_num * (1.0 + 0.5 * turn) + gate_b * push
            for h in range(2):
                at = pl.ds(h * rows + s * half, half)
                slab[u, at, :] = jnp.concatenate([d_corr * refs[2 * h], d_corr * refs[2 * h + 1]], axis=0).astype(bf16)
                saved = warped_ref[r, d, at, :].astype(f32)
                for k in range(2):
                    part = d_corr * saved[k * G : (k + 1) * G]
                    own[2 * h + k] = part if own[2 * h + k] is None else own[2 * h + k] + part
        own_acc[...] += jnp.concatenate(own, axis=0)
        src_acc[...] += jnp.dot(slab[u], w_ref[d], preferred_element_type=f32)

    def use_copies(r):
        copies = [
            remote(
                uses_ref.at[c, r, :, lanes(along(j))], side_in.at[core, j - 1, r], side_send.at[r, j, c],
                side_recv.at[r, j, core], (2 * chip + c, along(j)))
            for j in (2, 1, 3)
            for c in range(2)
        ]
        copies.append(
            remote(
                uses_ref.at[1 - core, r, :, lanes(p)], mate_in.at[r], match_send.at[r], match_recv.at[r], (sibling, p)))
        return copies

    def send_uses(r):
        for copy in use_copies(r):
            copy.start()

    @pl.loop(0, views)
    def _(r):
        edges_in(slope_ext, r, slope_send, slope_recv)

        @pl.loop(0, planes)
        def _(d):
            grad_ref[d] = conv(slope_ext, taps_bwd, r, d, True)

        src_acc[...] = jnp.zeros_like(src_acc)
        own_acc[...] = jnp.zeros_like(own_acc)

        @pl.loop(0, planes // group)
        def _(step):
            for u in range(group):
                backward(r, step * group + u, u)

            @pl.when((step == 0) & (r > 0))
            def _():
                send_uses(r - 1)

            @pl.when((step == 0) & (r == 0))
            def _():
                send_edges(slope_ext, views - 2, slope_send, slope_recv)
                activate(views - 1)

            @pl.when((step == 1) & (r == 0))
            def _():
                send_edges(slope_ext, views - 1, slope_send, slope_recv)

        for h in range(2):
            uses_ref[h, r, 0:rows] = src_acc[h * rows : (h + 1) * rows].astype(bf16)
            uses_ref[h, r, rows:full] = own_acc[h * half : (h + 1) * half].astype(bf16)

    place = lax.broadcasted_iota(jnp.int32, (1, LANES), 1)
    named = jnp.full((1, LANES), -1, jnp.int32)
    for c in range(2):
        for r in range(views):
            first = (2 * chip + c) * views + r
            for s in range(per_view):
                named = jnp.where(place == c * 64 + r * uses + s, sources_ref[first, s], named)
            named = jnp.where(place == c * 64 + r * uses + per_view, first, named)
    count = views * uses
    owned = chips * views
    row = lax.broadcasted_iota(jnp.int32, (2 * owned, 2 * LANES), 0)
    goal = ((row % owned) // views) * (2 * views) + (row // owned) * views + row % views
    pick = (goal == jnp.concatenate([named, named], axis=1)).astype(bf16)

    send_uses(views - 1)

    @pl.loop(0, views)
    def _(r):
        for j in range(1, n_plane):
            for c in range(2):
                part = side_in.at[c, j - 1, r]
                remote(part, part, side_send.at[r, j, c], side_recv.at[r, j, c], (v, p)).wait_recv()
        remote(mate_in.at[r], mate_in.at[r], match_send.at[r], match_recv.at[r], (sibling, p)).wait_recv()
        mine = uses_ref[core, r, :, lanes(p)].astype(f32)
        for c in range(2):
            here = jnp.where(core == c, mine, mate_in[r].astype(f32))
            start = pl.multiple_of((c * views + r) * full, half)
            summed[pl.ds(start, full)] = (here + side_in[c, 0, r].astype(f32)) + (
                side_in[c, 1, r].astype(f32) + side_in[c, 2, r].astype(f32))

    gap = jnp.zeros((64 - count, LANES), f32)
    for at in range(half):
        stack = jnp.concatenate(
            [
                summed[pl.ds(at, count, stride=half), :], gap,
                summed[pl.ds(views * full + at, count, stride=half), :], gap,
            ],
            axis=0)
        high = stack.astype(bf16)
        low = (stack - high.astype(f32)).astype(bf16)
        dense[pl.ds(at, 2 * owned, stride=half), :] = jnp.dot(
            pick, jnp.concatenate([high, low], axis=0), preferred_element_type=f32)

    block = views * half

    def shift(j):
        return lax.rem(chip + j, chips)

    def back_copy(a, j):
        return remote(
            blocks.at[a, shift(j)], ring_in.at[a, chip], back_send.at[a, j], back_recv.at[a, j],
            (2 * shift(j) + core, p))

    for a in range(2):

        @pl.loop(1, chips)
        def _(j):
            start = pl.multiple_of((a * chips + shift(j)) * block, block)
            blocks[a, shift(j)] = dense[pl.ds(start, block), :].astype(bf16)

            @pl.when(j > 1)
            def _():
                back_copy(a, j - 1).start()

        result[a] = dense[pl.ds(pl.multiple_of((a * chips + chip) * block, block), block), :]
        back_copy(a, chips - 1).start()

    def last_copies(a):
        return [
            remote(
                result.at[a], final_in.at[p, core], last_send.at[a, j], last_recv.at[j, core],
                (2 * chip + a, along(j)))
            for j in range(1, n_plane)
        ]

    def mate_copy():
        return remote(
            result.at[1 - core], final_in.at[p, core], last_send.at[1 - core, 0], last_recv.at[0, core], (sibling, p))

    for a in range(2):

        @pl.loop(1, chips)
        def _(j):
            origin = lax.rem(chip - j + chips, chips)
            part = ring_in.at[a, origin]
            remote(part, part, back_send.at[a, j], back_recv.at[a, j], (v, p)).wait_recv()
            result[a] += ring_in[a, origin].astype(f32)

        if a == 0:

            @pl.loop(1, chips)
            def _(j):
                back_copy(0, j).wait_send()

            for copy in last_copies(0):
                copy.start()

    final_in[p, core] = result[core]

    @pl.loop(1, chips)
    def _(j):
        back_copy(1, j).wait_send()

    for copy in last_copies(1):
        copy.start()
    mate_copy().start()

    for r in range(views):
        for copy in line_copies(r) + use_copies(r):
            copy.wait_send()

    def reorder(q):
        for h in range(2):
            for i in range(views):
                for k in range(2):
                    ordered[q, pl.ds(i * C + 2 * h + k, G, stride=GC), :] = final_in[q, h, pl.ds(i * half + k * G, G), :]
        for i in range(views):
            out_ref[i, :, lanes(q)] = ordered[q, i * C : (i + 1) * C, :]

    def last_arrived(j, h):
        q = along(-j)
        part = final_in.at[q, h]
        return remote(part, part, last_send.at[0, j], last_recv.at[j, h], (v, q))

    last_arrived(0, 1 - core).wait_recv()
    reorder(p)
    for j in (1, 3, 2):
        for h in range(2):
            last_arrived(j, h).wait_recv()
        reorder(along(-j))
    for a in range(2):
        for copy in last_copies(a):
            copy.wait_send()
    mate_copy().wait_send()


def shards(n_view, n_plane, features, sources, warp_weights, view_gate, depth_kernel, cotangent):
    views, channels, pixels = features.shape
    per_view = sources.shape[1]
    planes = warp_weights.shape[0]
    chips = n_view // 2
    half = channels // 2
    rows = per_view * half
    full = rows + half
    group = 4
    dma = pltpu.SemaphoreType.DMA
    vmem = pl.BlockSpec(memory_space=pltpu.VMEM)
    return pl.pallas_call(
        functools.partial(sweep_kernel, (views, per_view, planes, pixels, n_view, n_plane, group)),
        in_specs=[vmem, pl.BlockSpec(memory_space=pltpu.SMEM), pl.BlockSpec(memory_space=pl.ANY), vmem, vmem, vmem],
        out_specs=[vmem, vmem],
        out_shape=[
            jax.ShapeDtypeStruct(cotangent.shape, bf16),
            jax.ShapeDtypeStruct(features.shape, f32),
        ],
        scratch_shapes=[
            pltpu.VMEM(warp_weights.shape, bf16),
            pltpu.VMEM(features.shape, bf16),
            pltpu.VMEM((n_view * views, half, LANES), bf16),
            pltpu.VMEM((2, views, rows, LANES), bf16),
            pltpu.VMEM((views, 2, rows, pixels), bf16),
            pltpu.VMEM((views, planes, 2 * rows, pixels), bf16),
            pltpu.VMEM((views, planes, per_view * G, pixels), f32),
            pltpu.VMEM((views, planes, 16, pixels), f32),
            pltpu.VMEM((planes + 2, views, G, pixels), f32),
            pltpu.VMEM((planes + 2, views, G, pixels), f32),
            pltpu.VMEM((planes, G, pixels), f32),
            pltpu.VMEM((3 * G, G, LANES), f32),
            pltpu.VMEM((3 * G, G, LANES), f32),
            pltpu.VMEM((group, 2 * rows, pixels), bf16),
            pltpu.VMEM((2 * rows, pixels), f32),
            pltpu.VMEM((channels, pixels), f32),
            pltpu.VMEM((2, views, full, pixels), bf16),
            pltpu.VMEM((2, n_plane - 1, views, full, LANES), bf16),
            pltpu.VMEM((views, full, LANES), bf16),
            pltpu.VMEM((2 * views * full, LANES), f32),
            pltpu.VMEM((2 * chips * views * half, LANES), f32),
            pltpu.VMEM((2, chips, views * half, LANES), bf16),
            pltpu.VMEM((2, chips, views * half, LANES), bf16),
            pltpu.VMEM((2, views * half, LANES), f32),
            pltpu.VMEM((n_plane, 2, views * half, LANES), f32),
            pltpu.VMEM((n_plane, views * channels, LANES), f32),
            dma,
            dma((n_view,)), dma((n_view,)),
            dma((views, n_plane, 2)), dma((views, n_plane, 2)), dma((views,)), dma((views,)),
            dma((views, 2)), dma((views, 2)), dma((views, 2)), dma((views, 2)),
            dma((views, n_plane, 2)), dma((views, n_plane, 2)), dma((views,)), dma((views,)),
            dma((2, chips)), dma((2, chips)), dma((2, n_plane)), dma((n_plane, 2)),
        ],
        compiler_params=pltpu.CompilerParams(collective_id=0, has_side_effects=True),
        name="plane_sweep",
    )(features, sources, warp_weights, view_gate.reshape(1, G), depth_kernel, cotangent)


def solution(mesh):
    in_specs = (
        P("view", None, None),
        P(),
        P("plane", None, None),
        P(),
        P(),
        P("view", "plane", None, None),
    )
    out_specs = (P("view", "plane", None, None), P("view", None, None))
    body = functools.partial(shards, mesh.shape["view"], mesh.shape["plane"])
    return jax.shard_map(body, mesh=mesh, in_specs=in_specs, out_specs=out_specs, check_vma=False)
```

```python
import functools

import jax
import jax.numpy as jnp
from jax import lax
from jax.experimental import pallas as pl
from jax.experimental.pallas import tpu as pltpu
from jax.sharding import PartitionSpec as P

G = 8
GC = 4
C = G * GC
LANES = 128
MESH = pl.DeviceIdType.MESH
f32 = jnp.float32
bf16 = jnp.bfloat16


def column(row):
    eye = lax.broadcasted_iota(jnp.int32, (G, G), 0) == lax.broadcasted_iota(jnp.int32, (G, G), 1)
    return jnp.sum(jnp.where(eye, jnp.broadcast_to(row, (G, G)), 0.0), axis=1, keepdims=True)


def greet(peers):
    barrier = pltpu.get_barrier_semaphore()
    for peer in peers:
        pl.semaphore_signal(barrier, inc=1, device_id=peer, device_id_type=MESH)
    pl.semaphore_wait(barrier, len(peers))


def sweep_kernel(
    dims,
    feat_ref, sources_ref, w_hbm, gate_ref, taps_ref, cot_ref,
    regular_ref, out_ref,
    w_ref, refs_ref, pool, select, tiles_ref, warped_ref, corr_ref, aux_ref, cost_ext, slope_ext, grad_ref, taps_fwd, taps_bwd,
    slab, src_acc, own_acc, uses_ref, side_in, mate_in, summed, dense, blocks, ring_in, result, final_in, ordered,
    w_sem, ring_send, ring_recv, line_send, line_recv, mate_send, mate_recv,
    cost_send, cost_recv, slope_send, slope_recv,
    side_send, side_recv, match_send, match_recv, back_send, back_recv, last_send, last_recv,
):
    views, per_view, planes, pixels, n_view, n_plane, group = dims
    v, p = lax.axis_index("view"), lax.axis_index("plane")
    core = lax.rem(v, 2)
    chip = v // 2
    sibling = v + 1 - 2 * core
    chips = n_view // 2
    half = C // 2
    rows = per_view * half
    uses = per_view + 1
    full = uses * half

    def lanes(q):
        return pl.ds(pl.multiple_of(q * LANES, LANES), LANES)

    def remote(src, dst, send, recv, device):
        return pltpu.make_async_remote_copy(
            src_ref=src, dst_ref=dst, send_sem=send, recv_sem=recv, device_id=device, device_id_type=MESH)

    def along(j):
        return lax.rem(p + j + n_plane, n_plane)

    weights = pltpu.make_async_copy(w_hbm, w_ref, w_sem)
    weights.start()

    into = lax.broadcasted_iota(jnp.int32, (C, C), 0)
    outof = lax.broadcasted_iota(jnp.int32, (C, C), 1)
    swap = (outof == (into % G) * GC + into // G).astype(bf16)
    for i in range(views):
        refs_ref[i] = jnp.dot(swap, feat_ref[i], preferred_element_type=f32).astype(bf16)
    pool[pl.ds(v * views, views)] = refs_ref[:, pl.ds(pl.multiple_of(core * half, half), half), lanes(p)]

    peers = [(lax.rem(v + j, n_view), p) for j in range(1, n_view)]
    peers += [(2 * chip + c, along(j)) for c in range(2) for j in range(1, n_plane)]
    greet(peers)

    def ring_copy(j):
        target = lax.rem(v + j, n_view)
        part = refs_ref.at[:, pl.ds(pl.multiple_of(lax.rem(target, 2) * half, half), half), lanes(p)]
        return remote(part, pool.at[pl.ds(v * views, views)], ring_send.at[j], ring_recv.at[j], (target, p))

    def ring_arrived(j):
        owner = lax.rem(v - j + n_view, n_view)
        part = pool.at[pl.ds(owner * views, views)]
        return remote(part, part, ring_send.at[j], ring_recv.at[j], (owner, p))

    @pl.loop(1, n_view)
    def _(j):
        ring_copy(j).start()

    for k in range(3):
        taps = taps_ref[k]
        for g in range(G):
            taps_fwd[k * G + g] = jnp.broadcast_to(taps[:, g : g + 1], (G, LANES))
            taps_bwd[k * G + g] = jnp.broadcast_to(column(taps[g : g + 1, :]), (G, LANES))

    @pl.loop(1, n_view)
    def _(j):
        ring_arrived(j).wait_recv()

    def line_copies(r):
        copies = [
            remote(
                select.at[c, r], tiles_ref.at[r, core, :, lanes(p)], line_send.at[r, j, c], line_recv.at[r, j, core],
                (2 * chip + c, along(j)))
            for j in (2, 1, 3)
            for c in range(2)
        ]
        copies.append(
            remote(
                select.at[1 - core, r], tiles_ref.at[r, core, :, lanes(p)], mate_send.at[r], mate_recv.at[r],
                (sibling, p)))
        return copies

    def start_maps(r):
        for copy in line_copies(r):
            copy.start()

    def maps_left(r):
        for copy in line_copies(r):
            copy.wait_send()

    def maps_arrived(r):
        for j in range(1, n_plane):
            for h in range(2):
                part = tiles_ref.at[r, h, :, lanes(along(-j))]
                remote(part, part, line_send.at[r, j, h], line_recv.at[r, j, h], (v, along(-j))).wait_recv()
        part = tiles_ref.at[r, 1 - core, :, lanes(p)]
        remote(part, part, mate_send.at[r], mate_recv.at[r], (sibling, p)).wait_recv()

    for r in range(views):

        @pl.loop(0, per_view)
        def _(s):
            start = pl.multiple_of(s * half, half)
            for c in range(2):
                select[c, r, pl.ds(start, half)] = pool[sources_ref[s, (2 * chip + c) * views + r]]
            tiles_ref[r, core, pl.ds(start, half), lanes(p)] = pool[sources_ref[s, v * views + r]]

        if r == 1:
            start_maps(0)

    @pl.loop(1, n_view)
    def _(j):
        ring_copy(j).wait_send()

    maps_left(0)
    start_maps(1)
    maps_left(1)
    start_maps(2)

    def edges(buffer, r, send, recv):
        return (
            remote(buffer.at[1, r], buffer.at[planes + 1, r], send.at[r, 0], recv.at[r, 0], (v, along(-1))),
            remote(buffer.at[planes, r], buffer.at[0, r], send.at[r, 1], recv.at[r, 1], (v, along(1))),
        )

    def send_edges(buffer, r, send, recv):
        for copy in edges(buffer, r, send, recv):
            copy.start()

    gate_col = column(gate_ref[...])

    def pieces(maps, s):
        at = s * half
        return maps[at : at + G], maps[at + G : at + half], maps[rows + at : rows + at + G], maps[rows + at + G : rows + at + half]

    def forward(r, d):
        gate_b = jnp.broadcast_to(gate_col * 0.125, (G, pixels))
        warped = lax.dot_general(
            tiles_ref[r].reshape(2 * rows, pixels),
            w_ref[d],
            (((1,), (1,)), ((), ())),
            preferred_element_type=f32,
        )
        warped_ref[r, d] = warped.astype(bf16)
        ref_map = refs_ref[r].astype(f32)
        refs = [ref_map[k * G : (k + 1) * G] for k in range(GC)]
        weighted = None
        for s in range(per_view):
            terms = [one * ref for one, ref in zip(pieces(warped, s), refs)]
            corr = (terms[0] + terms[1]) + (terms[2] + terms[3])
            corr_ref[r, d, s * G : (s + 1) * G, :] = corr
            logit = jnp.sum(corr * gate_b, axis=0, keepdims=True)
            turn = jnp.tanh(logit)
            aux_ref[r, d, s : s + 1, :] = turn
            visible = 1.0 + 0.5 * turn
            if weighted is None:
                weighted = visible * corr
                total = visible
            else:
                weighted = weighted + visible * corr
                total = total + visible
        inverse = 1.0 / total
        aux_ref[r, d, per_view : per_view + 1, :] = inverse
        cost_ext[d + 1, r] = weighted * (inverse * 0.25)

    def conv(buffer, taps, r, d, flip):
        total = [None] * (pixels // LANES)
        for k in range(3):
            at = d + (2 - k if flip else k)
            for g in range(G):
                tap = taps[k * G + g]
                for t in range(pixels // LANES):
                    row = buffer[at, r, g : g + 1, t * LANES : (t + 1) * LANES]
                    term = tap * jnp.broadcast_to(row, (G, LANES))
                    total[t] = term if total[t] is None else total[t] + term
        return jnp.concatenate(total, axis=1)

    def edges_in(buffer, r, send, recv):
        for copy in edges(buffer, r, send, recv):
            copy.wait()
        buffer[0, r] = buffer[0, r] * jnp.where(p == 0, 0.0, 1.0)
        buffer[planes + 1, r] = buffer[planes + 1, r] * jnp.where(p == n_plane - 1, 0.0, 1.0)

    def activate(r):
        edges_in(cost_ext, r, cost_send, cost_recv)

        @pl.loop(0, planes)
        def _(d):
            pre = conv(cost_ext, taps_fwd, r, d, False)
            gate = jax.nn.sigmoid(pre)
            regular_ref[r, d] = (pre * gate).astype(bf16)
            slope_ext[d + 1, r] = cot_ref[r, d].astype(f32) * (gate * (1.0 + pre * (1.0 - gate)))

    weights.wait()

    @pl.loop(0, views)
    def _(r):
        maps_arrived(r)

        @pl.loop(0, planes // group)
        def _(step):
            for u in range(group):
                at = step * group + u
                forward(r, jnp.where(at == 0, 0, jnp.where(at == 1, planes - 1, at - 1)))

            @pl.when((step == 0) & (r == 0))
            def _():
                maps_left(2)
                start_maps(3)

            @pl.when((step == 0) & (r > 1))
            def _():
                activate(r - 2)

            @pl.when(step == 1)
            def _():
                send_edges(cost_ext, r, cost_send, cost_recv)

            @pl.when((step == 1) & (r > 1))
            def _():
                send_edges(slope_ext, r - 2, slope_send, slope_recv)

    activate(views - 2)

    def backward(r, d, u):
        gate_b = jnp.broadcast_to(gate_col * 0.0625, (G, pixels))
        ref_map = refs_ref[r].astype(f32)
        refs = [ref_map[k * G : (k + 1) * G] for k in range(GC)]
        inverse = aux_ref[r, d, per_view : per_view + 1, :]
        d_num = grad_ref[d] * (inverse * 0.25)
        cost4 = cost_ext[d + 1, r] * 4.0
        own = [None] * GC
        for s in range(per_view):
            corr = corr_ref[r, d, s * G : (s + 1) * G, :]
            turn = aux_ref[r, d, s : s + 1, :]
            push = jnp.sum(d_num * (corr - cost4), axis=0, keepdims=True)
            push = push * (1.0 - turn * turn)
            d_corr = d_num * (1.0 + 0.5 * turn) + gate_b * push
            for h in range(2):
                at = pl.ds(h * rows + s * half, half)
                slab[u, at, :] = jnp.concatenate([d_corr * refs[2 * h], d_corr * refs[2 * h + 1]], axis=0).astype(bf16)
                saved = warped_ref[r, d, at, :].astype(f32)
                for k in range(2):
                    part = d_corr * saved[k * G : (k + 1) * G]
                    own[2 * h + k] = part if own[2 * h + k] is None else own[2 * h + k] + part
        own_acc[...] += jnp.concatenate(own, axis=0)
        src_acc[...] += jnp.dot(slab[u], w_ref[d], preferred_element_type=f32)

    def use_copies(r):
        copies = [
            remote(
                uses_ref.at[c, r, :, lanes(along(j))], side_in.at[core, j - 1, r], side_send.at[r, j, c],
                side_recv.at[r, j, core], (2 * chip + c, along(j)))
            for j in (2, 1, 3)
            for c in range(2)
        ]
        copies.append(
            remote(
                uses_ref.at[1 - core, r, :, lanes(p)], mate_in.at[r], match_send.at[r], match_recv.at[r], (sibling, p)))
        return copies

    def send_uses(r):
        for copy in use_copies(r):
            copy.start()

    @pl.loop(0, views)
    def _(r):
        edges_in(slope_ext, r, slope_send, slope_recv)

        @pl.loop(0, planes)
        def _(d):
            grad_ref[d] = conv(slope_ext, taps_bwd, r, d, True)

        src_acc[...] = jnp.zeros_like(src_acc)
        own_acc[...] = jnp.zeros_like(own_acc)

        @pl.loop(0, planes // group)
        def _(step):
            for u in range(group):
                backward(r, step * group + u, u)

            @pl.when((step == 0) & (r > 0))
            def _():
                send_uses(r - 1)

            @pl.when((step == 0) & (r == 0))
            def _():
                send_edges(slope_ext, views - 2, slope_send, slope_recv)
                activate(views - 1)

            @pl.when((step == 1) & (r == 0))
            def _():
                send_edges(slope_ext, views - 1, slope_send, slope_recv)

        for h in range(2):
            uses_ref[h, r, 0:rows] = src_acc[h * rows : (h + 1) * rows].astype(bf16)
            uses_ref[h, r, rows:full] = own_acc[h * half : (h + 1) * half].astype(bf16)

    place = lax.broadcasted_iota(jnp.int32, (1, LANES), 1)
    named = jnp.full((1, LANES), -1, jnp.int32)
    for c in range(2):
        for r in range(views):
            first = (2 * chip + c) * views + r
            for s in range(per_view):
                named = jnp.where(place == c * 64 + r * uses + s, sources_ref[s, first], named)
            named = jnp.where(place == c * 64 + r * uses + per_view, first, named)
    count = views * uses
    owned = chips * views
    row = lax.broadcasted_iota(jnp.int32, (2 * owned, 2 * LANES), 0)
    goal = ((row % owned) // views) * (2 * views) + (row // owned) * views + row % views
    pick = (goal == jnp.concatenate([named, named], axis=1)).astype(bf16)

    send_uses(views - 1)

    @pl.loop(0, views)
    def _(r):
        for j in range(1, n_plane):
            for c in range(2):
                part = side_in.at[c, j - 1, r]
                remote(part, part, side_send.at[r, j, c], side_recv.at[r, j, c], (v, p)).wait_recv()
        remote(mate_in.at[r], mate_in.at[r], match_send.at[r], match_recv.at[r], (sibling, p)).wait_recv()
        mine = uses_ref[core, r, :, lanes(p)].astype(f32)
        for c in range(2):
            here = jnp.where(core == c, mine, mate_in[r].astype(f32))
            start = pl.multiple_of((c * views + r) * full, half)
            summed[pl.ds(start, full)] = (here + side_in[c, 0, r].astype(f32)) + (
                side_in[c, 1, r].astype(f32) + side_in[c, 2, r].astype(f32))

    gap = jnp.zeros((64 - count, LANES), f32)
    for at in range(half):
        stack = jnp.concatenate(
            [
                summed[pl.ds(at, count, stride=half), :], gap,
                summed[pl.ds(views * full + at, count, stride=half), :], gap,
            ],
            axis=0)
        high = stack.astype(bf16)
        low = (stack - high.astype(f32)).astype(bf16)
        dense[pl.ds(at, 2 * owned, stride=half), :] = jnp.dot(
            pick, jnp.concatenate([high, low], axis=0), preferred_element_type=f32)

    block = views * half

    def shift(j):
        return lax.rem(chip + j, chips)

    def back_copy(j):
        return remote(
            blocks.at[shift(j)], ring_in.at[chip], back_send.at[j], back_recv.at[j], (2 * shift(j) + core, p))

    def dense_block(a, u):
        return dense[pl.ds(pl.multiple_of((a * chips + u) * block, block), block), :]

    @pl.loop(1, chips)
    def _(j):
        for a in range(2):
            blocks[shift(j), a] = dense_block(a, shift(j)).astype(bf16)

        @pl.when(j > 1)
        def _():
            back_copy(j - 1).start()

    for a in range(2):
        result[a] = dense_block(a, chip)
    back_copy(chips - 1).start()

    def last_copies(a):
        return [
            remote(
                result.at[a], final_in.at[p, core], last_send.at[a, j], last_recv.at[j, core],
                (2 * chip + a, along(j)))
            for j in range(1, n_plane)
        ]

    def mate_copy():
        return remote(
            result.at[1 - core], final_in.at[p, core], last_send.at[1 - core, 0], last_recv.at[0, core], (sibling, p))

    @pl.loop(1, chips)
    def _(j):
        origin = lax.rem(chip - j + chips, chips)
        part = ring_in.at[origin]
        remote(part, part, back_send.at[j], back_recv.at[j], (v, p)).wait_recv()
        result[...] += ring_in[origin].astype(f32)

    final_in[p, core] = result[core]

    @pl.loop(1, chips)
    def _(j):
        back_copy(j).wait_send()

    for a in range(2):
        for copy in last_copies(a):
            copy.start()
    mate_copy().start()

    for r in range(views):
        for copy in use_copies(r):
            copy.wait_send()
    maps_left(views - 1)

    def reorder(q):
        for h in range(2):
            for i in range(views):
                for k in range(2):
                    ordered[q, pl.ds(i * C + 2 * h + k, G, stride=GC), :] = final_in[q, h, pl.ds(i * half + k * G, G), :]
        for i in range(views):
            out_ref[i, :, lanes(q)] = ordered[q, i * C : (i + 1) * C, :]

    def last_arrived(j, h):
        q = along(-j)
        part = final_in.at[q, h]
        return remote(part, part, last_send.at[0, j], last_recv.at[j, h], (v, q))

    last_arrived(0, 1 - core).wait_recv()
    reorder(p)
    for j in (1, 3, 2):
        for h in range(2):
            last_arrived(j, h).wait_recv()
        reorder(along(-j))
    for a in range(2):
        for copy in last_copies(a):
            copy.wait_send()
    mate_copy().wait_send()


def shards(n_view, n_plane, features, sources, warp_weights, view_gate, depth_kernel, cotangent):
    views, channels, pixels = features.shape
    per_view = sources.shape[1]
    planes = warp_weights.shape[0]
    chips = n_view // 2
    half = channels // 2
    rows = per_view * half
    full = rows + half
    group = 6
    dma = pltpu.SemaphoreType.DMA
    vmem = pl.BlockSpec(memory_space=pltpu.VMEM)
    return pl.pallas_call(
        functools.partial(sweep_kernel, (views, per_view, planes, pixels, n_view, n_plane, group)),
        in_specs=[vmem, pl.BlockSpec(memory_space=pltpu.SMEM), pl.BlockSpec(memory_space=pl.ANY), vmem, vmem, vmem],
        out_specs=[vmem, vmem],
        out_shape=[
            pltpu.VMEM(cotangent.shape, bf16),
            pltpu.VMEM(features.shape, f32),
        ],
        scratch_shapes=[
            pltpu.VMEM(warp_weights.shape, bf16),
            pltpu.VMEM(features.shape, bf16),
            pltpu.VMEM((n_view * views, half, LANES), bf16),
            pltpu.VMEM((2, views, rows, LANES), bf16),
            pltpu.VMEM((views, 2, rows, pixels), bf16),
            pltpu.VMEM((views, planes, 2 * rows, pixels), bf16),
            pltpu.VMEM((views, planes, per_view * G, pixels), f32),
            pltpu.VMEM((views, planes, 16, pixels), f32),
            pltpu.VMEM((planes + 2, views, G, pixels), f32),
            pltpu.VMEM((planes + 2, views, G, pixels), f32),
            pltpu.VMEM((planes, G, pixels), f32),
            pltpu.VMEM((3 * G, G, LANES), f32),
            pltpu.VMEM((3 * G, G, LANES), f32),
            pltpu.VMEM((group, 2 * rows, pixels), bf16),
            pltpu.VMEM((2 * rows, pixels), f32),
            pltpu.VMEM((channels, pixels), f32),
            pltpu.VMEM((2, views, full, pixels), bf16),
            pltpu.VMEM((2, n_plane - 1, views, full, LANES), bf16),
            pltpu.VMEM((views, full, LANES), bf16),
            pltpu.VMEM((2 * views * full, LANES), f32),
            pltpu.VMEM((2 * chips * views * half, LANES), f32),
            pltpu.VMEM((chips, 2, views * half, LANES), bf16),
            pltpu.VMEM((chips, 2, views * half, LANES), bf16),
            pltpu.VMEM((2, views * half, LANES), f32),
            pltpu.VMEM((n_plane, 2, views * half, LANES), f32),
            pltpu.VMEM((n_plane, views * channels, LANES), f32),
            dma,
            dma((n_view,)), dma((n_view,)),
            dma((views, n_plane, 2)), dma((views, n_plane, 2)), dma((views,)), dma((views,)),
            dma((views, 2)), dma((views, 2)), dma((views, 2)), dma((views, 2)),
            dma((views, n_plane, 2)), dma((views, n_plane, 2)), dma((views,)), dma((views,)),
            dma((chips,)), dma((chips,)), dma((2, n_plane)), dma((n_plane, 2)),
        ],
        compiler_params=pltpu.CompilerParams(collective_id=0, has_side_effects=True),
        name="plane_sweep",
    )(features, sources.T, warp_weights, view_gate.reshape(1, G), depth_kernel, cotangent)


def solution(mesh):
    in_specs = (
        P("view", None, None),
        P(),
        P("plane", None, None),
        P(),
        P(),
        P("view", "plane", None, None),
    )
    out_specs = (P("view", "plane", None, None), P("view", None, None))
    body = functools.partial(shards, mesh.shape["view"], mesh.shape["plane"])
    return jax.shard_map(body, mesh=mesh, in_specs=in_specs, out_specs=out_specs, check_vma=False)
```

```python
import functools

import jax
import jax.numpy as jnp
from jax import lax
from jax.experimental import pallas as pl
from jax.experimental.pallas import tpu as pltpu
from jax.sharding import PartitionSpec as P

G = 8
GC = 4
C = G * GC
LANES = 128
MESH = pl.DeviceIdType.MESH
f32 = jnp.float32
bf16 = jnp.bfloat16


def column(row):
    eye = lax.broadcasted_iota(jnp.int32, (G, G), 0) == lax.broadcasted_iota(jnp.int32, (G, G), 1)
    return jnp.sum(jnp.where(eye, jnp.broadcast_to(row, (G, G)), 0.0), axis=1, keepdims=True)


def greet(peers):
    for peer in peers:
        pl.semaphore_signal(pltpu.get_barrier_semaphore(), inc=1, device_id=peer, device_id_type=MESH)


def sweep_kernel(
    dims,
    feat_ref, sources_ref, w_hbm, gate_ref, taps_ref, cot_hbm,
    regular_ref, out_ref,
    w_ref, cot_ref, refs_ref, pool, select, tiles_ref, warped_ref, corr_ref, aux_ref, cost_ext, slope_ext, grad_ref, taps_fwd, taps_bwd,
    slab, src_acc, own_acc, uses_ref, side_in, mate_in, summed, dense, blocks, ring_in, result, final_in, ordered,
    w_sem, cot_sem, ring_send, ring_recv, line_send, line_recv, mate_send, mate_recv,
    cost_send, cost_recv, slope_send, slope_recv,
    side_send, side_recv, match_send, match_recv, back_send, back_recv, last_send, last_recv,
):
    views, per_view, planes, pixels, n_view, n_plane, group = dims
    v, p = lax.axis_index("view"), lax.axis_index("plane")
    core = lax.rem(v, 2)
    chip = v // 2
    sibling = v + 1 - 2 * core
    chips = n_view // 2
    half = C // 2
    rows = per_view * half
    uses = per_view + 1
    full = uses * half

    def lanes(q):
        return pl.ds(pl.multiple_of(q * LANES, LANES), LANES)

    def remote(src, dst, send, recv, device):
        return pltpu.make_async_remote_copy(
            src_ref=src, dst_ref=dst, send_sem=send, recv_sem=recv, device_id=device, device_id_type=MESH)

    def along(j):
        return lax.rem(p + j + n_plane, n_plane)

    weights = pltpu.make_async_copy(w_hbm, w_ref, w_sem)
    weights.start()
    cotangents = pltpu.make_async_copy(cot_hbm, cot_ref, cot_sem)
    cotangents.start()

    peers = [(lax.rem(v + j, n_view), p) for j in range(1, n_view)]
    peers += [(2 * chip + c, along(j)) for c in range(2) for j in range(1, n_plane)]
    greet(peers)

    into = lax.broadcasted_iota(jnp.int32, (C, C), 0)
    outof = lax.broadcasted_iota(jnp.int32, (C, C), 1)
    swap = (outof == (into % G) * GC + into // G).astype(bf16)
    for i in range(views):
        refs_ref[i] = jnp.dot(swap, feat_ref[i], preferred_element_type=f32).astype(bf16)
    pool[pl.ds(v * views, views)] = refs_ref[:, pl.ds(pl.multiple_of(core * half, half), half), lanes(p)]

    pl.semaphore_wait(pltpu.get_barrier_semaphore(), len(peers))

    def ring_copy(j):
        target = lax.rem(v + j, n_view)
        part = refs_ref.at[:, pl.ds(pl.multiple_of(lax.rem(target, 2) * half, half), half), lanes(p)]
        return remote(part, pool.at[pl.ds(v * views, views)], ring_send.at[j], ring_recv.at[j], (target, p))

    def ring_arrived(j):
        owner = lax.rem(v - j + n_view, n_view)
        part = pool.at[pl.ds(owner * views, views)]
        return remote(part, part, ring_send.at[j], ring_recv.at[j], (owner, p))

    @pl.loop(1, n_view)
    def _(j):
        ring_copy(j).start()

    for k in range(3):
        taps = taps_ref[k]
        for g in range(G):
            taps_fwd[k * G + g] = jnp.broadcast_to(taps[:, g : g + 1], (G, LANES))
            taps_bwd[k * G + g] = jnp.broadcast_to(column(taps[g : g + 1, :]), (G, LANES))

    @pl.loop(1, n_view)
    def _(j):
        ring_arrived(j).wait_recv()

    def line_copies(r):
        copies = [
            remote(
                select.at[c, r], tiles_ref.at[r, core, :, lanes(p)], line_send.at[r, j, c], line_recv.at[r, j, core],
                (2 * chip + c, along(j)))
            for j in (2, 1, 3)
            for c in range(2)
        ]
        copies.append(
            remote(
                select.at[1 - core, r], tiles_ref.at[r, core, :, lanes(p)], mate_send.at[r], mate_recv.at[r],
                (sibling, p)))
        return copies

    def start_maps(r):
        for copy in line_copies(r):
            copy.start()

    def maps_arrived(r):
        for j in range(1, n_plane):
            for h in range(2):
                part = tiles_ref.at[r, h, :, lanes(along(-j))]
                remote(part, part, line_send.at[r, j, h], line_recv.at[r, j, h], (v, along(-j))).wait_recv()
        part = tiles_ref.at[r, 1 - core, :, lanes(p)]
        remote(part, part, mate_send.at[r], mate_recv.at[r], (sibling, p)).wait_recv()

    for r in range(views):

        @pl.loop(0, per_view)
        def _(s):
            start = pl.multiple_of(s * half, half)
            for c in range(2):
                select[c, r, pl.ds(start, half)] = pool[sources_ref[s, (2 * chip + c) * views + r]]
            tiles_ref[r, core, pl.ds(start, half), lanes(p)] = pool[sources_ref[s, v * views + r]]

        if r > 0:
            start_maps(r - 1)

    @pl.loop(1, n_view)
    def _(j):
        ring_copy(j).wait_send()

    start_maps(views - 1)

    def edges(buffer, r, send, recv):
        return (
            remote(buffer.at[1, r], buffer.at[planes + 1, r], send.at[r, 0], recv.at[r, 0], (v, along(-1))),
            remote(buffer.at[planes, r], buffer.at[0, r], send.at[r, 1], recv.at[r, 1], (v, along(1))),
        )

    def send_edges(buffer, r, send, recv):
        for copy in edges(buffer, r, send, recv):
            copy.start()

    gate_col = column(gate_ref[...])

    def pieces(maps, s):
        at = s * half
        return maps[at : at + G], maps[at + G : at + half], maps[rows + at : rows + at + G], maps[rows + at + G : rows + at + half]

    def forward(r, d):
        gate_b = jnp.broadcast_to(gate_col * 0.125, (G, pixels))
        warped = lax.dot_general(
            tiles_ref[r].reshape(2 * rows, pixels),
            w_ref[d],
            (((1,), (1,)), ((), ())),
            preferred_element_type=f32,
        )
        warped_ref[r, d] = warped.astype(bf16)
        ref_map = refs_ref[r].astype(f32)
        refs = [ref_map[k * G : (k + 1) * G] for k in range(GC)]
        weighted = None
        for s in range(per_view):
            terms = [one * ref for one, ref in zip(pieces(warped, s), refs)]
            corr = (terms[0] + terms[1]) + (terms[2] + terms[3])
            corr_ref[r, d, s * G : (s + 1) * G, :] = corr
            logit = jnp.sum(corr * gate_b, axis=0, keepdims=True)
            turn = jnp.tanh(logit)
            aux_ref[r, d, s : s + 1, :] = turn
            visible = 1.0 + 0.5 * turn
            if weighted is None:
                weighted = visible * corr
                total = visible
            else:
                weighted = weighted + visible * corr
                total = total + visible
        inverse = 1.0 / total
        aux_ref[r, d, per_view : per_view + 1, :] = inverse
        cost_ext[d + 1, r] = weighted * (inverse * 0.25)

    def conv(buffer, taps, r, d, flip):
        total = [None] * (pixels // LANES)
        for k in range(3):
            at = d + (2 - k if flip else k)
            for g in range(G):
                tap = taps[k * G + g]
                for t in range(pixels // LANES):
                    row = buffer[at, r, g : g + 1, t * LANES : (t + 1) * LANES]
                    term = tap * jnp.broadcast_to(row, (G, LANES))
                    total[t] = term if total[t] is None else total[t] + term
        return jnp.concatenate(total, axis=1)

    def edges_in(buffer, r, send, recv):
        for copy in edges(buffer, r, send, recv):
            copy.wait()
        buffer[0, r] = buffer[0, r] * jnp.where(p == 0, 0.0, 1.0)
        buffer[planes + 1, r] = buffer[planes + 1, r] * jnp.where(p == n_plane - 1, 0.0, 1.0)

    def activate(r):
        edges_in(cost_ext, r, cost_send, cost_recv)

        @pl.loop(0, planes)
        def _(d):
            pre = conv(cost_ext, taps_fwd, r, d, False)
            gate = jax.nn.sigmoid(pre)
            regular_ref[r, d] = (pre * gate).astype(bf16)
            slope_ext[d + 1, r] = cot_ref[r, d].astype(f32) * (gate * (1.0 + pre * (1.0 - gate)))

    weights.wait()
    cotangents.wait()

    @pl.loop(0, views)
    def _(r):
        maps_arrived(r)

        @pl.loop(0, planes // group)
        def _(step):
            for u in range(group):
                at = step * group + u
                forward(r, jnp.where(at == 0, 0, jnp.where(at == 1, planes - 1, at - 1)))

            @pl.when((step == 0) & (r > 1))
            def _():
                activate(r - 2)

            @pl.when(step == 1)
            def _():
                send_edges(cost_ext, r, cost_send, cost_recv)

            @pl.when((step == 1) & (r > 1))
            def _():
                send_edges(slope_ext, r - 2, slope_send, slope_recv)

    activate(views - 2)

    def backward(r, d, u):
        gate_b = jnp.broadcast_to(gate_col * 0.0625, (G, pixels))
        ref_map = refs_ref[r].astype(f32)
        refs = [ref_map[k * G : (k + 1) * G] for k in range(GC)]
        inverse = aux_ref[r, d, per_view : per_view + 1, :]
        d_num = grad_ref[d] * (inverse * 0.25)
        cost4 = cost_ext[d + 1, r] * 4.0
        own = [None] * GC
        for s in range(per_view):
            corr = corr_ref[r, d, s * G : (s + 1) * G, :]
            turn = aux_ref[r, d, s : s + 1, :]
            push = jnp.sum(d_num * (corr - cost4), axis=0, keepdims=True)
            push = push * (1.0 - turn * turn)
            d_corr = d_num * (1.0 + 0.5 * turn) + gate_b * push
            for h in range(2):
                at = pl.ds(h * rows + s * half, half)
                slab[u, at, :] = jnp.concatenate([d_corr * refs[2 * h], d_corr * refs[2 * h + 1]], axis=0).astype(bf16)
                saved = warped_ref[r, d, at, :].astype(f32)
                for k in range(2):
                    part = d_corr * saved[k * G : (k + 1) * G]
                    own[2 * h + k] = part if own[2 * h + k] is None else own[2 * h + k] + part
        own_acc[...] += jnp.concatenate(own, axis=0)
        src_acc[...] += jnp.dot(slab[u], w_ref[d], preferred_element_type=f32)

    def use_copies(r):
        copies = [
            remote(
                uses_ref.at[c, r, :, lanes(along(j))], side_in.at[core, j - 1, r], side_send.at[r, j, c],
                side_recv.at[r, j, core], (2 * chip + c, along(j)))
            for j in (2, 1, 3)
            for c in range(2)
        ]
        copies.append(
            remote(
                uses_ref.at[1 - core, r, :, lanes(p)], mate_in.at[r], match_send.at[r], match_recv.at[r], (sibling, p)))
        return copies

    def send_uses(r):
        for copy in use_copies(r):
            copy.start()

    @pl.loop(0, views)
    def _(r):
        edges_in(slope_ext, r, slope_send, slope_recv)

        @pl.loop(0, planes)
        def _(d):
            grad_ref[d] = conv(slope_ext, taps_bwd, r, d, True)

        @pl.when(r > 0)
        def _():
            send_uses(r - 1)

        src_acc[...] = jnp.zeros_like(src_acc)
        own_acc[...] = jnp.zeros_like(own_acc)

        @pl.loop(0, planes // group)
        def _(step):
            for u in range(group):
                backward(r, step * group + u, u)

            @pl.when((step == 0) & (r == 0))
            def _():
                send_edges(slope_ext, views - 2, slope_send, slope_recv)
                activate(views - 1)

            @pl.when((step == 1) & (r == 0))
            def _():
                send_edges(slope_ext, views - 1, slope_send, slope_recv)

        for h in range(2):
            uses_ref[h, r, 0:rows] = src_acc[h * rows : (h + 1) * rows].astype(bf16)
            uses_ref[h, r, rows:full] = own_acc[h * half : (h + 1) * half].astype(bf16)

    place = lax.broadcasted_iota(jnp.int32, (1, LANES), 1)
    named = jnp.full((1, LANES), -1, jnp.int32)
    for c in range(2):
        for r in range(views):
            first = (2 * chip + c) * views + r
            for s in range(per_view):
                named = jnp.where(place == c * 64 + r * uses + s, sources_ref[s, first], named)
            named = jnp.where(place == c * 64 + r * uses + per_view, first, named)
    count = views * uses
    owned = chips * views
    row = lax.broadcasted_iota(jnp.int32, (2 * owned, 2 * LANES), 0)
    goal = ((row % owned) // views) * (2 * views) + (row // owned) * views + row % views
    pick = (goal == jnp.concatenate([named, named], axis=1)).astype(bf16)

    send_uses(views - 1)

    @pl.loop(0, views)
    def _(r):
        for j in range(1, n_plane):
            for c in range(2):
                part = side_in.at[c, j - 1, r]
                remote(part, part, side_send.at[r, j, c], side_recv.at[r, j, c], (v, p)).wait_recv()
        remote(mate_in.at[r], mate_in.at[r], match_send.at[r], match_recv.at[r], (sibling, p)).wait_recv()
        mine = uses_ref[core, r, :, lanes(p)].astype(f32)
        for c in range(2):
            here = jnp.where(core == c, mine, mate_in[r].astype(f32))
            start = pl.multiple_of((c * views + r) * full, half)
            summed[pl.ds(start, full)] = (here + side_in[c, 0, r].astype(f32)) + (
                side_in[c, 1, r].astype(f32) + side_in[c, 2, r].astype(f32))

    gap = jnp.zeros((64 - count, LANES), f32)
    for at in range(half):
        stack = jnp.concatenate(
            [
                summed[pl.ds(at, count, stride=half), :], gap,
                summed[pl.ds(views * full + at, count, stride=half), :], gap,
            ],
            axis=0)
        high = stack.astype(bf16)
        low = (stack - high.astype(f32)).astype(bf16)
        dense[pl.ds(at, 2 * owned, stride=half), :] = jnp.dot(
            pick, jnp.concatenate([high, low], axis=0), preferred_element_type=f32)

    block = views * half

    def shift(j):
        return lax.rem(chip + j, chips)

    def back_copy(j):
        return remote(
            blocks.at[shift(j)], ring_in.at[chip], back_send.at[j], back_recv.at[j], (2 * shift(j) + core, p))

    def dense_block(a, u):
        return dense[pl.ds(pl.multiple_of((a * chips + u) * block, block), block), :]

    @pl.loop(1, chips)
    def _(j):
        for a in range(2):
            blocks[shift(j), a] = dense_block(a, shift(j)).astype(bf16)

        @pl.when(j > 1)
        def _():
            back_copy(j - 1).start()

    for a in range(2):
        result[a] = dense_block(a, chip)
    back_copy(chips - 1).start()

    def last_copies(a):
        return [
            remote(
                result.at[a], final_in.at[p, core], last_send.at[a, j], last_recv.at[j, core],
                (2 * chip + a, along(j)))
            for j in range(1, n_plane)
        ]

    def mate_copy():
        return remote(
            result.at[1 - core], final_in.at[p, core], last_send.at[1 - core, 0], last_recv.at[0, core], (sibling, p))

    @pl.loop(1, chips)
    def _(j):
        origin = lax.rem(chip - j + chips, chips)
        part = ring_in.at[origin]
        remote(part, part, back_send.at[j], back_recv.at[j], (v, p)).wait_recv()
        result[...] += ring_in[origin].astype(f32)

    final_in[p, core] = result[core]

    @pl.loop(1, chips)
    def _(j):
        back_copy(j).wait_send()

    for a in range(2):
        for copy in last_copies(a):
            copy.start()
    mate_copy().start()

    for r in range(views):
        for copy in line_copies(r) + use_copies(r):
            copy.wait_send()

    def reorder(q):
        for h in range(2):
            for i in range(views):
                for k in range(2):
                    ordered[q, pl.ds(i * C + 2 * h + k, G, stride=GC), :] = final_in[q, h, pl.ds(i * half + k * G, G), :]
        for i in range(views):
            out_ref[i, :, lanes(q)] = ordered[q, i * C : (i + 1) * C, :]

    def last_arrived(j, h):
        q = along(-j)
        part = final_in.at[q, h]
        return remote(part, part, last_send.at[0, j], last_recv.at[j, h], (v, q))

    last_arrived(0, 1 - core).wait_recv()
    reorder(p)
    for j in (1, 3, 2):
        for h in range(2):
            last_arrived(j, h).wait_recv()
        reorder(along(-j))
    for a in range(2):
        for copy in last_copies(a):
            copy.wait_send()
    mate_copy().wait_send()


def shards(n_view, n_plane, features, sources, warp_weights, view_gate, depth_kernel, cotangent):
    views, channels, pixels = features.shape
    per_view = sources.shape[1]
    planes = warp_weights.shape[0]
    chips = n_view // 2
    half = channels // 2
    rows = per_view * half
    full = rows + half
    group = 6
    dma = pltpu.SemaphoreType.DMA
    vmem = pl.BlockSpec(memory_space=pltpu.VMEM)
    return pl.pallas_call(
        functools.partial(sweep_kernel, (views, per_view, planes, pixels, n_view, n_plane, group)),
        in_specs=[vmem, pl.BlockSpec(memory_space=pltpu.SMEM), pl.BlockSpec(memory_space=pl.ANY), vmem, vmem, pl.BlockSpec(memory_space=pl.ANY)],
        out_specs=[vmem, vmem],
        out_shape=[
            pltpu.VMEM(cotangent.shape, bf16),
            pltpu.VMEM(features.shape, f32),
        ],
        scratch_shapes=[
            pltpu.VMEM(warp_weights.shape, bf16),
            pltpu.VMEM(cotangent.shape, bf16),
            pltpu.VMEM(features.shape, bf16),
            pltpu.VMEM((n_view * views, half, LANES), bf16),
            pltpu.VMEM((2, views, rows, LANES), bf16),
            pltpu.VMEM((views, 2, rows, pixels), bf16),
            pltpu.VMEM((views, planes, 2 * rows, pixels), bf16),
            pltpu.VMEM((views, planes, per_view * G, pixels), f32),
            pltpu.VMEM((views, planes, 16, pixels), f32),
            pltpu.VMEM((planes + 2, views, G, pixels), f32),
            pltpu.VMEM((planes + 2, views, G, pixels), f32),
            pltpu.VMEM((planes, G, pixels), f32),
            pltpu.VMEM((3 * G, G, LANES), f32),
            pltpu.VMEM((3 * G, G, LANES), f32),
            pltpu.VMEM((group, 2 * rows, pixels), bf16),
            pltpu.VMEM((2 * rows, pixels), f32),
            pltpu.VMEM((channels, pixels), f32),
            pltpu.VMEM((2, views, full, pixels), bf16),
            pltpu.VMEM((2, n_plane - 1, views, full, LANES), bf16),
            pltpu.VMEM((views, full, LANES), bf16),
            pltpu.VMEM((2 * views * full, LANES), f32),
            pltpu.VMEM((2 * chips * views * half, LANES), f32),
            pltpu.VMEM((chips, 2, views * half, LANES), bf16),
            pltpu.VMEM((chips, 2, views * half, LANES), bf16),
            pltpu.VMEM((2, views * half, LANES), f32),
            pltpu.VMEM((n_plane, 2, views * half, LANES), f32),
            pltpu.VMEM((n_plane, views * channels, LANES), f32),
            dma, dma,
            dma((n_view,)), dma((n_view,)),
            dma((views, n_plane, 2)), dma((views, n_plane, 2)), dma((views,)), dma((views,)),
            dma((views, 2)), dma((views, 2)), dma((views, 2)), dma((views, 2)),
            dma((views, n_plane, 2)), dma((views, n_plane, 2)), dma((views,)), dma((views,)),
            dma((chips,)), dma((chips,)), dma((2, n_plane)), dma((n_plane, 2)),
        ],
        compiler_params=pltpu.CompilerParams(collective_id=0, has_side_effects=True),
        name="plane_sweep",
    )(features, sources.T, warp_weights, view_gate.reshape(1, G), depth_kernel, cotangent)


def solution(mesh):
    in_specs = (
        P("view", None, None),
        P(),
        P("plane", None, None),
        P(),
        P(),
        P("view", "plane", None, None),
    )
    out_specs = (P("view", "plane", None, None), P("view", None, None))
    body = functools.partial(shards, mesh.shape["view"], mesh.shape["plane"])
    return jax.shard_map(body, mesh=mesh, in_specs=in_specs, out_specs=out_specs, check_vma=False)
```

```python
import functools

import jax
import jax.numpy as jnp
from jax import lax
from jax.experimental import pallas as pl
from jax.experimental.pallas import tpu as pltpu
from jax.sharding import PartitionSpec as P

G = 8
GC = 4
C = G * GC
LANES = 128
MESH = pl.DeviceIdType.MESH
f32 = jnp.float32
bf16 = jnp.bfloat16


def column(row):
    eye = lax.broadcasted_iota(jnp.int32, (G, G), 0) == lax.broadcasted_iota(jnp.int32, (G, G), 1)
    return jnp.sum(jnp.where(eye, jnp.broadcast_to(row, (G, G)), 0.0), axis=1, keepdims=True)


def greet(peers):
    for peer in peers:
        pl.semaphore_signal(pltpu.get_barrier_semaphore(), inc=1, device_id=peer, device_id_type=MESH)


def sweep_kernel(
    dims,
    feat_ref, sources_ref, w_hbm, gate_ref, taps_ref, cot_hbm,
    regular_ref, out_ref,
    w_ref, cot_ref, refs_ref, pool, select, tiles_ref, warped_ref, corr_ref, aux_ref, cost_ext, slope_ext, grad_ref, taps_fwd, taps_bwd,
    slab, src_acc, own_acc, uses_ref, side_in, mate_in, summed, dense, blocks, ring_in, result, final_in, ordered,
    w_sem, cot_sem, ring_send, ring_recv, line_send, line_recv, mate_send, mate_recv,
    cost_send, cost_recv, slope_send, slope_recv,
    side_send, side_recv, match_send, match_recv, back_send, back_recv, last_send, last_recv,
):
    views, per_view, planes, pixels, n_view, n_plane = dims
    v, p = lax.axis_index("view"), lax.axis_index("plane")
    core = lax.rem(v, 2)
    chip = v // 2
    sibling = v + 1 - 2 * core
    chips = n_view // 2
    half = C // 2
    rows = per_view * half
    uses = per_view + 1
    full = uses * half

    def lanes(q):
        return pl.ds(pl.multiple_of(q * LANES, LANES), LANES)

    def remote(src, dst, send, recv, device):
        return pltpu.make_async_remote_copy(
            src_ref=src, dst_ref=dst, send_sem=send, recv_sem=recv, device_id=device, device_id_type=MESH)

    def along(j):
        return lax.rem(p + j + n_plane, n_plane)

    weights = pltpu.make_async_copy(w_hbm, w_ref, w_sem)
    weights.start()
    cotangents = pltpu.make_async_copy(cot_hbm, cot_ref, cot_sem)
    cotangents.start()

    peers = [(lax.rem(v + j, n_view), p) for j in range(1, n_view)]
    peers += [(2 * chip + c, along(j)) for c in range(2) for j in range(1, n_plane)]
    greet(peers)

    into = lax.broadcasted_iota(jnp.int32, (C, C), 0)
    outof = lax.broadcasted_iota(jnp.int32, (C, C), 1)
    swap = (outof == (into % G) * GC + into // G).astype(bf16)
    for i in range(views):
        refs_ref[i] = jnp.dot(swap, feat_ref[i], preferred_element_type=f32).astype(bf16)
    pool[pl.ds(v * views, views)] = refs_ref[:, pl.ds(pl.multiple_of(core * half, half), half), lanes(p)]

    pl.semaphore_wait(pltpu.get_barrier_semaphore(), len(peers))

    def ring_copy(j):
        target = lax.rem(v + j, n_view)
        part = refs_ref.at[:, pl.ds(pl.multiple_of(lax.rem(target, 2) * half, half), half), lanes(p)]
        return remote(part, pool.at[pl.ds(v * views, views)], ring_send.at[j], ring_recv.at[j], (target, p))

    def ring_arrived(j):
        owner = lax.rem(v - j + n_view, n_view)
        part = pool.at[pl.ds(owner * views, views)]
        return remote(part, part, ring_send.at[j], ring_recv.at[j], (owner, p))

    @pl.loop(1, n_view)
    def _(j):
        ring_copy(j).start()

    for k in range(3):
        taps = taps_ref[k]
        for g in range(G):
            taps_fwd[k * G + g] = jnp.broadcast_to(taps[:, g : g + 1], (G, LANES))
            taps_bwd[k * G + g] = jnp.broadcast_to(column(taps[g : g + 1, :]), (G, LANES))

    @pl.loop(1, n_view)
    def _(j):
        ring_arrived(j).wait_recv()

    def line_copies(r):
        copies = [
            remote(
                select.at[c, r], tiles_ref.at[r, core, :, lanes(p)], line_send.at[r, j, c], line_recv.at[r, j, core],
                (2 * chip + c, along(j)))
            for j in (2, 1, 3)
            for c in range(2)
        ]
        copies.append(
            remote(
                select.at[1 - core, r], tiles_ref.at[r, core, :, lanes(p)], mate_send.at[r], mate_recv.at[r],
                (sibling, p)))
        return copies

    def start_maps(r):
        for copy in line_copies(r):
            copy.start()

    def maps_arrived(r):
        for j in range(1, n_plane):
            for h in range(2):
                part = tiles_ref.at[r, h, :, lanes(along(-j))]
                remote(part, part, line_send.at[r, j, h], line_recv.at[r, j, h], (v, along(-j))).wait_recv()
        part = tiles_ref.at[r, 1 - core, :, lanes(p)]
        remote(part, part, mate_send.at[r], mate_recv.at[r], (sibling, p)).wait_recv()

    for r in range(views):

        @pl.loop(0, per_view)
        def _(s):
            start = pl.multiple_of(s * half, half)
            for c in range(2):
                select[c, r, pl.ds(start, half)] = pool[sources_ref[s, (2 * chip + c) * views + r]]
            tiles_ref[r, core, pl.ds(start, half), lanes(p)] = pool[sources_ref[s, v * views + r]]

        if r > 0:
            start_maps(r - 1)

    @pl.loop(1, n_view)
    def _(j):
        ring_copy(j).wait_send()

    start_maps(views - 1)

    def edges(buffer, r, send, recv):
        return (
            remote(buffer.at[1, r], buffer.at[planes + 1, r], send.at[r, 0], recv.at[r, 0], (v, along(-1))),
            remote(buffer.at[planes, r], buffer.at[0, r], send.at[r, 1], recv.at[r, 1], (v, along(1))),
        )

    def send_edges(buffer, r, send, recv):
        for copy in edges(buffer, r, send, recv):
            copy.start()

    gate_col = column(gate_ref[...])

    def pieces(maps, s):
        at = s * half
        return maps[at : at + G], maps[at + G : at + half], maps[rows + at : rows + at + G], maps[rows + at + G : rows + at + half]

    def forward(r, d):
        gate_b = jnp.broadcast_to(gate_col * 0.125, (G, pixels))
        warped = lax.dot_general(
            tiles_ref[r].reshape(2 * rows, pixels),
            w_ref[d],
            (((1,), (1,)), ((), ())),
            preferred_element_type=f32,
        )
        warped_ref[r, d] = warped.astype(bf16)
        ref_map = refs_ref[r].astype(f32)
        refs = [ref_map[k * G : (k + 1) * G] for k in range(GC)]
        weighted = None
        for s in range(per_view):
            terms = [one * ref for one, ref in zip(pieces(warped, s), refs)]
            corr = (terms[0] + terms[1]) + (terms[2] + terms[3])
            corr_ref[r, d, s * G : (s + 1) * G, :] = corr
            logit = jnp.sum(corr * gate_b, axis=0, keepdims=True)
            turn = jnp.tanh(logit)
            aux_ref[r, d, s : s + 1, :] = turn
            visible = 1.0 + 0.5 * turn
            if weighted is None:
                weighted = visible * corr
                total = visible
            else:
                weighted = weighted + visible * corr
                total = total + visible
        inverse = 1.0 / total
        aux_ref[r, d, per_view : per_view + 1, :] = inverse
        cost_ext[d + 1, r] = weighted * (inverse * 0.25)

    def conv(buffer, taps, r, d, flip):
        total = [None] * (pixels // LANES)
        for k in range(3):
            at = d + (2 - k if flip else k)
            for g in range(G):
                tap = taps[k * G + g]
                for t in range(pixels // LANES):
                    row = buffer[at, r, g : g + 1, t * LANES : (t + 1) * LANES]
                    term = tap * jnp.broadcast_to(row, (G, LANES))
                    total[t] = term if total[t] is None else total[t] + term
        return jnp.concatenate(total, axis=1)

    def edges_in(buffer, r, send, recv):
        for copy in edges(buffer, r, send, recv):
            copy.wait()
        buffer[0, r] = buffer[0, r] * jnp.where(p == 0, 0.0, 1.0)
        buffer[planes + 1, r] = buffer[planes + 1, r] * jnp.where(p == n_plane - 1, 0.0, 1.0)

    def activate(r):
        edges_in(cost_ext, r, cost_send, cost_recv)

        @pl.loop(0, planes, unroll=4)
        def _(d):
            pre = conv(cost_ext, taps_fwd, r, d, False)
            gate = jax.nn.sigmoid(pre)
            regular_ref[r, d] = (pre * gate).astype(bf16)
            slope_ext[d + 1, r] = cot_ref[r, d].astype(f32) * (gate * (1.0 + pre * (1.0 - gate)))

    weights.wait()
    cotangents.wait()

    @pl.loop(0, views)
    def _(r):
        maps_arrived(r)

        @pl.when(r > 0)
        def _():
            send_edges(cost_ext, r - 1, cost_send, cost_recv)

        @pl.when(r > 2)
        def _():
            send_edges(slope_ext, r - 3, slope_send, slope_recv)

        for d in range(planes):
            forward(r, d)

        @pl.when(r > 1)
        def _():
            activate(r - 2)

    send_edges(cost_ext, views - 1, cost_send, cost_recv)
    activate(views - 2)
    send_edges(slope_ext, views - 3, slope_send, slope_recv)

    def backward(r, d, u):
        gate_b = jnp.broadcast_to(gate_col * 0.0625, (G, pixels))
        ref_map = refs_ref[r].astype(f32)
        refs = [ref_map[k * G : (k + 1) * G] for k in range(GC)]
        inverse = aux_ref[r, d, per_view : per_view + 1, :]
        d_num = grad_ref[d] * (inverse * 0.25)
        cost4 = cost_ext[d + 1, r] * 4.0
        own = [None] * GC
        for s in range(per_view):
            corr = corr_ref[r, d, s * G : (s + 1) * G, :]
            turn = aux_ref[r, d, s : s + 1, :]
            push = jnp.sum(d_num * (corr - cost4), axis=0, keepdims=True)
            push = push * (1.0 - turn * turn)
            d_corr = d_num * (1.0 + 0.5 * turn) + gate_b * push
            for h in range(2):
                at = pl.ds(h * rows + s * half, half)
                slab[u, at, :] = jnp.concatenate([d_corr * refs[2 * h], d_corr * refs[2 * h + 1]], axis=0).astype(bf16)
                saved = warped_ref[r, d, at, :].astype(f32)
                for k in range(2):
                    part = d_corr * saved[k * G : (k + 1) * G]
                    own[2 * h + k] = part if own[2 * h + k] is None else own[2 * h + k] + part
        own_acc[...] += jnp.concatenate(own, axis=0)
        src_acc[...] += jnp.dot(slab[u], w_ref[d], preferred_element_type=f32)

    def use_copies(r):
        copies = [
            remote(
                uses_ref.at[c, r, :, lanes(along(j))], side_in.at[core, j - 1, r], side_send.at[r, j, c],
                side_recv.at[r, j, core], (2 * chip + c, along(j)))
            for j in (2, 1, 3)
            for c in range(2)
        ]
        copies.append(
            remote(
                uses_ref.at[1 - core, r, :, lanes(p)], mate_in.at[r], match_send.at[r], match_recv.at[r], (sibling, p)))
        return copies

    def send_uses(r):
        for copy in use_copies(r):
            copy.start()

    @pl.loop(0, views)
    def _(r):
        edges_in(slope_ext, r, slope_send, slope_recv)

        @pl.loop(0, planes, unroll=4)
        def _(d):
            grad_ref[d] = conv(slope_ext, taps_bwd, r, d, True)

        @pl.when(r > 0)
        def _():
            send_uses(r - 1)

        @pl.when(r < 2)
        def _():
            send_edges(slope_ext, views - 2 + r, slope_send, slope_recv)

        src_acc[...] = jnp.zeros_like(src_acc)
        own_acc[...] = jnp.zeros_like(own_acc)

        for d in range(planes):
            backward(r, d, d)

        @pl.when(r == 0)
        def _():
            activate(views - 1)

        for h in range(2):
            uses_ref[h, r, 0:rows] = src_acc[h * rows : (h + 1) * rows].astype(bf16)
            uses_ref[h, r, rows:full] = own_acc[h * half : (h + 1) * half].astype(bf16)

    place = lax.broadcasted_iota(jnp.int32, (1, LANES), 1)
    named = jnp.full((1, LANES), -1, jnp.int32)
    for c in range(2):
        for r in range(views):
            first = (2 * chip + c) * views + r
            for s in range(per_view):
                named = jnp.where(place == c * 64 + r * uses + s, sources_ref[s, first], named)
            named = jnp.where(place == c * 64 + r * uses + per_view, first, named)
    count = views * uses
    owned = chips * views
    row = lax.broadcasted_iota(jnp.int32, (2 * owned, 2 * LANES), 0)
    goal = ((row % owned) // views) * (2 * views) + (row // owned) * views + row % views
    pick = (goal == jnp.concatenate([named, named], axis=1)).astype(bf16)

    send_uses(views - 1)

    @pl.loop(0, views)
    def _(r):
        for j in range(1, n_plane):
            for c in range(2):
                part = side_in.at[c, j - 1, r]
                remote(part, part, side_send.at[r, j, c], side_recv.at[r, j, c], (v, p)).wait_recv()
        remote(mate_in.at[r], mate_in.at[r], match_send.at[r], match_recv.at[r], (sibling, p)).wait_recv()
        mine = uses_ref[core, r, :, lanes(p)].astype(f32)
        for c in range(2):
            here = jnp.where(core == c, mine, mate_in[r].astype(f32))
            start = pl.multiple_of((c * views + r) * full, half)
            summed[pl.ds(start, full)] = (here + side_in[c, 0, r].astype(f32)) + (
                side_in[c, 1, r].astype(f32) + side_in[c, 2, r].astype(f32))

    gap = jnp.zeros((64 - count, LANES), f32)
    for at in range(half):
        stack = jnp.concatenate(
            [
                summed[pl.ds(at, count, stride=half), :], gap,
                summed[pl.ds(views * full + at, count, stride=half), :], gap,
            ],
            axis=0)
        high = stack.astype(bf16)
        low = (stack - high.astype(f32)).astype(bf16)
        dense[pl.ds(at, 2 * owned, stride=half), :] = jnp.dot(
            pick, jnp.concatenate([high, low], axis=0), preferred_element_type=f32)

    block = views * half

    def shift(j):
        return lax.rem(chip + j, chips)

    def back_copy(j):
        return remote(
            blocks.at[shift(j)], ring_in.at[chip], back_send.at[j], back_recv.at[j], (2 * shift(j) + core, p))

    def dense_block(a, u):
        return dense[pl.ds(pl.multiple_of((a * chips + u) * block, block), block), :]

    @pl.loop(1, chips)
    def _(j):
        for a in range(2):
            blocks[shift(j), a] = dense_block(a, shift(j)).astype(bf16)

        @pl.when(j > 1)
        def _():
            back_copy(j - 1).start()

    for a in range(2):
        result[a] = dense_block(a, chip)
    back_copy(chips - 1).start()

    def last_copies(a):
        return [
            remote(
                result.at[a], final_in.at[p, core], last_send.at[a, j], last_recv.at[j, core],
                (2 * chip + a, along(j)))
            for j in range(1, n_plane)
        ]

    def mate_copy():
        return remote(
            result.at[1 - core], final_in.at[p, core], last_send.at[1 - core, 0], last_recv.at[0, core], (sibling, p))

    @pl.loop(1, chips)
    def _(j):
        origin = lax.rem(chip - j + chips, chips)
        part = ring_in.at[origin]
        remote(part, part, back_send.at[j], back_recv.at[j], (v, p)).wait_recv()
        result[...] += ring_in[origin].astype(f32)

    final_in[p, core] = result[core]

    @pl.loop(1, chips)
    def _(j):
        back_copy(j).wait_send()

    for a in range(2):
        for copy in last_copies(a):
            copy.start()
    mate_copy().start()

    for r in range(views):
        for copy in line_copies(r) + use_copies(r):
            copy.wait_send()

    def reorder(q):
        for h in range(2):
            for i in range(views):
                for k in range(2):
                    ordered[q, pl.ds(i * C + 2 * h + k, G, stride=GC), :] = final_in[q, h, pl.ds(i * half + k * G, G), :]
        for i in range(views):
            out_ref[i, :, lanes(q)] = ordered[q, i * C : (i + 1) * C, :]

    def last_arrived(j, h):
        q = along(-j)
        part = final_in.at[q, h]
        return remote(part, part, last_send.at[0, j], last_recv.at[j, h], (v, q))

    last_arrived(0, 1 - core).wait_recv()
    reorder(p)
    for j in (1, 3, 2):
        for h in range(2):
            last_arrived(j, h).wait_recv()
        reorder(along(-j))
    for a in range(2):
        for copy in last_copies(a):
            copy.wait_send()
    mate_copy().wait_send()


def shards(n_view, n_plane, features, sources, warp_weights, view_gate, depth_kernel, cotangent):
    views, channels, pixels = features.shape
    per_view = sources.shape[1]
    planes = warp_weights.shape[0]
    chips = n_view // 2
    half = channels // 2
    rows = per_view * half
    full = rows + half
    dma = pltpu.SemaphoreType.DMA
    vmem = pl.BlockSpec(memory_space=pltpu.VMEM)
    return pl.pallas_call(
        functools.partial(sweep_kernel, (views, per_view, planes, pixels, n_view, n_plane)),
        in_specs=[vmem, pl.BlockSpec(memory_space=pltpu.SMEM), pl.BlockSpec(memory_space=pl.ANY), vmem, vmem, pl.BlockSpec(memory_space=pl.ANY)],
        out_specs=[vmem, vmem],
        out_shape=[
            pltpu.VMEM(cotangent.shape, bf16),
            pltpu.VMEM(features.shape, f32),
        ],
        scratch_shapes=[
            pltpu.VMEM(warp_weights.shape, bf16),
            pltpu.VMEM(cotangent.shape, bf16),
            pltpu.VMEM(features.shape, bf16),
            pltpu.VMEM((n_view * views, half, LANES), bf16),
            pltpu.VMEM((2, views, rows, LANES), bf16),
            pltpu.VMEM((views, 2, rows, pixels), bf16),
            pltpu.VMEM((views, planes, 2 * rows, pixels), bf16),
            pltpu.VMEM((views, planes, per_view * G, pixels), f32),
            pltpu.VMEM((views, planes, 16, pixels), f32),
            pltpu.VMEM((planes + 2, views, G, pixels), f32),
            pltpu.VMEM((planes + 2, views, G, pixels), f32),
            pltpu.VMEM((planes, G, pixels), f32),
            pltpu.VMEM((3 * G, G, LANES), f32),
            pltpu.VMEM((3 * G, G, LANES), f32),
            pltpu.VMEM((planes, 2 * rows, pixels), bf16),
            pltpu.VMEM((2 * rows, pixels), f32),
            pltpu.VMEM((channels, pixels), f32),
            pltpu.VMEM((2, views, full, pixels), bf16),
            pltpu.VMEM((2, n_plane - 1, views, full, LANES), bf16),
            pltpu.VMEM((views, full, LANES), bf16),
            pltpu.VMEM((2 * views * full, LANES), f32),
            pltpu.VMEM((2 * chips * views * half, LANES), f32),
            pltpu.VMEM((chips, 2, views * half, LANES), bf16),
            pltpu.VMEM((chips, 2, views * half, LANES), bf16),
            pltpu.VMEM((2, views * half, LANES), f32),
            pltpu.VMEM((n_plane, 2, views * half, LANES), f32),
            pltpu.VMEM((n_plane, views * channels, LANES), f32),
            dma, dma,
            dma((n_view,)), dma((n_view,)),
            dma((views, n_plane, 2)), dma((views, n_plane, 2)), dma((views,)), dma((views,)),
            dma((views, 2)), dma((views, 2)), dma((views, 2)), dma((views, 2)),
            dma((views, n_plane, 2)), dma((views, n_plane, 2)), dma((views,)), dma((views,)),
            dma((chips,)), dma((chips,)), dma((2, n_plane)), dma((n_plane, 2)),
        ],
        compiler_params=pltpu.CompilerParams(collective_id=0, has_side_effects=True),
        name="plane_sweep",
    )(features, sources.T, warp_weights, view_gate.reshape(1, G), depth_kernel, cotangent)


def solution(mesh):
    in_specs = (
        P("view", None, None),
        P(),
        P("plane", None, None),
        P(),
        P(),
        P("view", "plane", None, None),
    )
    out_specs = (P("view", "plane", None, None), P("view", None, None))
    body = functools.partial(shards, mesh.shape["view"], mesh.shape["plane"])
    return jax.shard_map(body, mesh=mesh, in_specs=in_specs, out_specs=out_specs, check_vma=False)
```

```python
import functools

import jax
import jax.numpy as jnp
from jax import lax
from jax.experimental import pallas as pl
from jax.experimental.pallas import tpu as pltpu
from jax.sharding import PartitionSpec as P

G = 8
GC = 4
C = G * GC
LANES = 128
MESH = pl.DeviceIdType.MESH
f32 = jnp.float32
bf16 = jnp.bfloat16


def column(row):
    eye = lax.broadcasted_iota(jnp.int32, (G, G), 0) == lax.broadcasted_iota(jnp.int32, (G, G), 1)
    return jnp.sum(jnp.where(eye, jnp.broadcast_to(row, (G, G)), 0.0), axis=1, keepdims=True)


def greet(peers):
    for peer in peers:
        pl.semaphore_signal(pltpu.get_barrier_semaphore(), inc=1, device_id=peer, device_id_type=MESH)


def sweep_kernel(
    dims,
    feat_ref, sources_ref, w_hbm, gate_ref, taps_ref, cot_hbm,
    regular_ref, out_ref,
    w_ref, cot_ref, refs_ref, pool, select, tiles_ref, warped_ref, corr_ref, aux_ref, cost_ext, slope_ext, grad_ref, taps_fwd, taps_bwd,
    slab, src_acc, own_acc, uses_ref, side_in, mate_in, summed, dense, blocks, ring_in, result, finished, final_in, ordered, pick_ref,
    w_sem, cot_sem, ring_send, ring_recv, line_send, line_recv, mate_send, mate_recv,
    cost_send, cost_recv, slope_send, slope_recv,
    side_send, side_recv, match_send, match_recv, back_send, back_recv, last_send, last_recv,
):
    views, per_view, planes, pixels, n_view, n_plane = dims
    v, p = lax.axis_index("view"), lax.axis_index("plane")
    core = lax.rem(v, 2)
    chip = v // 2
    sibling = v + 1 - 2 * core
    chips = n_view // 2
    half = C // 2
    rows = per_view * half
    uses = per_view + 1
    full = uses * half

    def lanes(q):
        return pl.ds(pl.multiple_of(q * LANES, LANES), LANES)

    def remote(src, dst, send, recv, device):
        return pltpu.make_async_remote_copy(
            src_ref=src, dst_ref=dst, send_sem=send, recv_sem=recv, device_id=device, device_id_type=MESH)

    def along(j):
        return lax.rem(p + j + n_plane, n_plane)

    weights = pltpu.make_async_copy(w_hbm, w_ref, w_sem)
    weights.start()
    cotangents = pltpu.make_async_copy(cot_hbm, cot_ref, cot_sem)
    cotangents.start()

    peers = [(lax.rem(v + j, n_view), p) for j in range(1, n_view)]
    peers += [(2 * chip + c, along(j)) for c in range(2) for j in range(1, n_plane)]
    greet(peers)

    into = lax.broadcasted_iota(jnp.int32, (C, C), 0)
    outof = lax.broadcasted_iota(jnp.int32, (C, C), 1)
    swap = (outof == (into % G) * GC + into // G).astype(bf16)
    for i in range(views):
        refs_ref[i] = jnp.dot(swap, feat_ref[i], preferred_element_type=f32).astype(bf16)
    pool[pl.ds(v * views, views)] = refs_ref[:, pl.ds(pl.multiple_of(core * half, half), half), lanes(p)]

    pl.semaphore_wait(pltpu.get_barrier_semaphore(), len(peers))

    def ring_copy(j):
        target = lax.rem(v + j, n_view)
        part = refs_ref.at[:, pl.ds(pl.multiple_of(lax.rem(target, 2) * half, half), half), lanes(p)]
        return remote(part, pool.at[pl.ds(v * views, views)], ring_send.at[j], ring_recv.at[j], (target, p))

    def ring_arrived(j):
        owner = lax.rem(v - j + n_view, n_view)
        part = pool.at[pl.ds(owner * views, views)]
        return remote(part, part, ring_send.at[j], ring_recv.at[j], (owner, p))

    @pl.loop(1, n_view)
    def _(j):
        ring_copy(j).start()

    for k in range(3):
        taps = taps_ref[k]
        for g in range(G):
            taps_fwd[k * G + g] = jnp.broadcast_to(taps[:, g : g + 1], (G, LANES))
            taps_bwd[k * G + g] = jnp.broadcast_to(column(taps[g : g + 1, :]), (G, LANES))

    place = lax.broadcasted_iota(jnp.int32, (1, LANES), 1)
    named = jnp.full((1, LANES), -1, jnp.int32)
    for c in range(2):
        for r in range(views):
            first = (2 * chip + c) * views + r
            for s in range(per_view):
                named = jnp.where(place == c * 64 + r * uses + s, sources_ref[s, first], named)
            named = jnp.where(place == c * 64 + r * uses + per_view, first, named)
    count = views * uses
    owned = chips * views
    row = lax.broadcasted_iota(jnp.int32, (2 * owned, 2 * LANES), 0)
    goal = ((row % owned) // views) * (2 * views) + (row // owned) * views + row % views
    pick_ref[...] = (goal == jnp.concatenate([named, named], axis=1)).astype(bf16)

    @pl.loop(1, n_view)
    def _(j):
        ring_arrived(j).wait_recv()

    def line_copies(r):
        copies = [
            remote(
                select.at[c, r], tiles_ref.at[r, core, :, lanes(p)], line_send.at[r, j, c], line_recv.at[r, j, core],
                (2 * chip + c, along(j)))
            for j in (2, 1, 3)
            for c in range(2)
        ]
        copies.append(
            remote(
                select.at[1 - core, r], tiles_ref.at[r, core, :, lanes(p)], mate_send.at[r], mate_recv.at[r],
                (sibling, p)))
        return copies

    def start_maps(r):
        for copy in line_copies(r):
            copy.start()

    def maps_arrived(r):
        for j in range(1, n_plane):
            for h in range(2):
                part = tiles_ref.at[r, h, :, lanes(along(-j))]
                remote(part, part, line_send.at[r, j, h], line_recv.at[r, j, h], (v, along(-j))).wait_recv()
        part = tiles_ref.at[r, 1 - core, :, lanes(p)]
        remote(part, part, mate_send.at[r], mate_recv.at[r], (sibling, p)).wait_recv()

    for r in range(views):

        @pl.loop(0, per_view)
        def _(s):
            start = pl.multiple_of(s * half, half)
            for c in range(2):
                select[c, r, pl.ds(start, half)] = pool[sources_ref[s, (2 * chip + c) * views + r]]
            tiles_ref[r, core, pl.ds(start, half), lanes(p)] = pool[sources_ref[s, v * views + r]]

        if r > 0:
            start_maps(r - 1)

    @pl.loop(1, n_view)
    def _(j):
        ring_copy(j).wait_send()

    start_maps(views - 1)

    def edges(buffer, r, send, recv):
        return (
            remote(buffer.at[1, r], buffer.at[planes + 1, r], send.at[r, 0], recv.at[r, 0], (v, along(-1))),
            remote(buffer.at[planes, r], buffer.at[0, r], send.at[r, 1], recv.at[r, 1], (v, along(1))),
        )

    def send_edges(buffer, r, send, recv):
        for copy in edges(buffer, r, send, recv):
            copy.start()

    gate_col = column(gate_ref[...])

    def pieces(maps, s):
        at = s * half
        return maps[at : at + G], maps[at + G : at + half], maps[rows + at : rows + at + G], maps[rows + at + G : rows + at + half]

    def forward(r, d):
        gate_b = jnp.broadcast_to(gate_col * 0.125, (G, pixels))
        warped = lax.dot_general(
            tiles_ref[r].reshape(2 * rows, pixels),
            w_ref[d],
            (((1,), (1,)), ((), ())),
            preferred_element_type=f32,
        )
        warped_ref[r, d] = warped.astype(bf16)
        ref_map = refs_ref[r].astype(f32)
        refs = [ref_map[k * G : (k + 1) * G] for k in range(GC)]
        weighted = None
        for s in range(per_view):
            terms = [one * ref for one, ref in zip(pieces(warped, s), refs)]
            corr = (terms[0] + terms[1]) + (terms[2] + terms[3])
            corr_ref[r, d, s * G : (s + 1) * G, :] = corr
            logit = jnp.sum(corr * gate_b, axis=0, keepdims=True)
            turn = jnp.tanh(logit)
            aux_ref[r, d, s : s + 1, :] = turn
            visible = 1.0 + 0.5 * turn
            if weighted is None:
                weighted = visible * corr
                total = visible
            else:
                weighted = weighted + visible * corr
                total = total + visible
        inverse = 1.0 / total
        aux_ref[r, d, per_view : per_view + 1, :] = inverse
        cost_ext[d + 1, r] = weighted * (inverse * 0.25)

    def conv(buffer, taps, r, d, flip):
        total = [None] * (pixels // LANES)
        for k in range(3):
            at = d + (2 - k if flip else k)
            for g in range(G):
                tap = taps[k * G + g]
                for t in range(pixels // LANES):
                    row = buffer[at, r, g : g + 1, t * LANES : (t + 1) * LANES]
                    term = tap * jnp.broadcast_to(row, (G, LANES))
                    total[t] = term if total[t] is None else total[t] + term
        return jnp.concatenate(total, axis=1)

    def edges_in(buffer, r, send, recv):
        for copy in edges(buffer, r, send, recv):
            copy.wait()
        buffer[0, r] = buffer[0, r] * jnp.where(p == 0, 0.0, 1.0)
        buffer[planes + 1, r] = buffer[planes + 1, r] * jnp.where(p == n_plane - 1, 0.0, 1.0)

    def activate(r):
        edges_in(cost_ext, r, cost_send, cost_recv)

        @pl.loop(0, planes, unroll=4)
        def _(d):
            pre = conv(cost_ext, taps_fwd, r, d, False)
            gate = jax.nn.sigmoid(pre)
            regular_ref[r, d] = (pre * gate).astype(bf16)
            slope_ext[d + 1, r] = cot_ref[r, d].astype(f32) * (gate * (1.0 + pre * (1.0 - gate)))

    weights.wait()
    cotangents.wait()

    @pl.loop(0, views)
    def _(r):
        maps_arrived(r)

        @pl.when(r > 0)
        def _():
            send_edges(cost_ext, r - 1, cost_send, cost_recv)

        @pl.when(r > 2)
        def _():
            send_edges(slope_ext, r - 3, slope_send, slope_recv)

        for d in range(planes):
            forward(r, d)

        @pl.when(r > 1)
        def _():
            activate(r - 2)

    send_edges(cost_ext, views - 1, cost_send, cost_recv)
    activate(views - 2)
    send_edges(slope_ext, views - 3, slope_send, slope_recv)

    def backward(r, d, u):
        gate_b = jnp.broadcast_to(gate_col * 0.0625, (G, pixels))
        ref_map = refs_ref[r].astype(f32)
        refs = [ref_map[k * G : (k + 1) * G] for k in range(GC)]
        inverse = aux_ref[r, d, per_view : per_view + 1, :]
        d_num = grad_ref[d] * (inverse * 0.25)
        cost4 = cost_ext[d + 1, r] * 4.0
        own = [None] * GC
        for s in range(per_view):
            corr = corr_ref[r, d, s * G : (s + 1) * G, :]
            turn = aux_ref[r, d, s : s + 1, :]
            push = jnp.sum(d_num * (corr - cost4), axis=0, keepdims=True)
            push = push * (1.0 - turn * turn)
            d_corr = d_num * (1.0 + 0.5 * turn) + gate_b * push
            for h in range(2):
                at = pl.ds(h * rows + s * half, half)
                slab[u, at, :] = jnp.concatenate([d_corr * refs[2 * h], d_corr * refs[2 * h + 1]], axis=0).astype(bf16)
                saved = warped_ref[r, d, at, :].astype(f32)
                for k in range(2):
                    part = d_corr * saved[k * G : (k + 1) * G]
                    own[2 * h + k] = part if own[2 * h + k] is None else own[2 * h + k] + part
        own_acc[...] += jnp.concatenate(own, axis=0)
        src_acc[...] += jnp.dot(slab[u], w_ref[d], preferred_element_type=f32)

    def use_copies(r):
        copies = [
            remote(
                uses_ref.at[c, r, :, lanes(along(j))], side_in.at[core, j - 1, r], side_send.at[r, j, c],
                side_recv.at[r, j, core], (2 * chip + c, along(j)))
            for j in (2, 1, 3)
            for c in range(2)
        ]
        copies.append(
            remote(
                uses_ref.at[1 - core, r, :, lanes(p)], mate_in.at[r], match_send.at[r], match_recv.at[r], (sibling, p)))
        return copies

    def send_uses(r):
        for copy in use_copies(r):
            copy.start()

    @pl.loop(0, views)
    def _(r):
        edges_in(slope_ext, r, slope_send, slope_recv)

        @pl.loop(0, planes, unroll=4)
        def _(d):
            grad_ref[d] = conv(slope_ext, taps_bwd, r, d, True)

        @pl.when(r > 0)
        def _():
            send_uses(r - 1)

        @pl.when(r < 2)
        def _():
            send_edges(slope_ext, views - 2 + r, slope_send, slope_recv)

        src_acc[...] = jnp.zeros_like(src_acc)
        own_acc[...] = jnp.zeros_like(own_acc)

        for d in range(planes):
            backward(r, d, d)

        @pl.when(r == 0)
        def _():
            activate(views - 1)

        for h in range(2):
            uses_ref[h, r, 0:rows] = src_acc[h * rows : (h + 1) * rows].astype(bf16)
            uses_ref[h, r, rows:full] = own_acc[h * half : (h + 1) * half].astype(bf16)

    for r in range(views):
        for copy in line_copies(r):
            copy.wait_send()

    send_uses(views - 1)

    @pl.loop(0, views)
    def _(r):
        for j in range(1, n_plane):
            for c in range(2):
                part = side_in.at[c, j - 1, r]
                remote(part, part, side_send.at[r, j, c], side_recv.at[r, j, c], (v, p)).wait_recv()
        remote(mate_in.at[r], mate_in.at[r], match_send.at[r], match_recv.at[r], (sibling, p)).wait_recv()
        mine = uses_ref[core, r, :, lanes(p)].astype(f32)
        for c in range(2):
            here = jnp.where(core == c, mine, mate_in[r].astype(f32))
            start = pl.multiple_of((c * views + r) * full, half)
            summed[pl.ds(start, full)] = (here + side_in[c, 0, r].astype(f32)) + (
                side_in[c, 1, r].astype(f32) + side_in[c, 2, r].astype(f32))

    gap = jnp.zeros((64 - count, LANES), f32)
    for at in range(half):
        stack = jnp.concatenate(
            [
                summed[pl.ds(at, count, stride=half), :], gap,
                summed[pl.ds(views * full + at, count, stride=half), :], gap,
            ],
            axis=0)
        high = stack.astype(bf16)
        low = (stack - high.astype(f32)).astype(bf16)
        dense[pl.ds(at, 2 * owned, stride=half), :] = jnp.dot(
            pick_ref[...], jnp.concatenate([high, low], axis=0), preferred_element_type=f32)

    block = views * half

    def shift(j):
        return lax.rem(chip + j, chips)

    def back_copy(j):
        return remote(
            blocks.at[shift(j)], ring_in.at[chip], back_send.at[j], back_recv.at[j], (2 * shift(j) + core, p))

    def dense_block(a, u):
        return dense[pl.ds(pl.multiple_of((a * chips + u) * block, block), block), :]

    @pl.loop(1, chips)
    def _(j):
        for a in range(2):
            blocks[shift(j), a] = dense_block(a, shift(j)).astype(bf16)

        @pl.when(j > 1)
        def _():
            back_copy(j - 1).start()

    for a in range(2):
        result[a] = dense_block(a, chip)
    back_copy(chips - 1).start()

    def last_copies(a):
        return [
            remote(
                finished.at[a], final_in.at[p, core], last_send.at[a, j], last_recv.at[j, core],
                (2 * chip + a, along(j)))
            for j in (2, 1, 3)
        ]

    def mate_copy():
        return remote(
            finished.at[1 - core], final_in.at[p, core], last_send.at[1 - core, 0], last_recv.at[0, core], (sibling, p))

    @pl.loop(1, chips)
    def _(j):
        origin = lax.rem(chip - j + chips, chips)
        part = ring_in.at[origin]
        remote(part, part, back_send.at[j], back_recv.at[j], (v, p)).wait_recv()
        result[...] += ring_in[origin].astype(f32)

    finished[...] = result[...].astype(bf16)
    final_in[p, core] = finished[core]

    @pl.loop(1, chips)
    def _(j):
        back_copy(j).wait_send()

    for a in range(2):
        for copy in last_copies(a):
            copy.start()
    mate_copy().start()

    for r in range(views):
        for copy in use_copies(r):
            copy.wait_send()

    def reorder(q):
        for h in range(2):
            piece = final_in[q, h].astype(f32)
            for i in range(views):
                for k in range(2):
                    at = i * half + k * G
                    ordered[q, pl.ds(i * C + 2 * h + k, G, stride=GC), :] = piece[at : at + G]
        for i in range(views):
            out_ref[i, :, lanes(q)] = ordered[q, i * C : (i + 1) * C, :]

    def last_arrived(j, h):
        q = along(-j)
        part = final_in.at[q, h]
        return remote(part, part, last_send.at[0, j], last_recv.at[j, h], (v, q))

    last_arrived(0, 1 - core).wait_recv()
    reorder(p)
    for j in (1, 3, 2):
        for h in range(2):
            last_arrived(j, h).wait_recv()
        reorder(along(-j))
    for a in range(2):
        for copy in last_copies(a):
            copy.wait_send()
    mate_copy().wait_send()


def shards(n_view, n_plane, features, sources, warp_weights, view_gate, depth_kernel, cotangent):
    views, channels, pixels = features.shape
    per_view = sources.shape[1]
    planes = warp_weights.shape[0]
    chips = n_view // 2
    half = channels // 2
    rows = per_view * half
    full = rows + half
    dma = pltpu.SemaphoreType.DMA
    vmem = pl.BlockSpec(memory_space=pltpu.VMEM)
    return pl.pallas_call(
        functools.partial(sweep_kernel, (views, per_view, planes, pixels, n_view, n_plane)),
        in_specs=[vmem, pl.BlockSpec(memory_space=pltpu.SMEM), pl.BlockSpec(memory_space=pl.ANY), vmem, vmem, pl.BlockSpec(memory_space=pl.ANY)],
        out_specs=[vmem, vmem],
        out_shape=[
            pltpu.VMEM(cotangent.shape, bf16),
            pltpu.VMEM(features.shape, f32),
        ],
        scratch_shapes=[
            pltpu.VMEM(warp_weights.shape, bf16),
            pltpu.VMEM(cotangent.shape, bf16),
            pltpu.VMEM(features.shape, bf16),
            pltpu.VMEM((n_view * views, half, LANES), bf16),
            pltpu.VMEM((2, views, rows, LANES), bf16),
            pltpu.VMEM((views, 2, rows, pixels), bf16),
            pltpu.VMEM((views, planes, 2 * rows, pixels), bf16),
            pltpu.VMEM((views, planes, per_view * G, pixels), f32),
            pltpu.VMEM((views, planes, 16, pixels), f32),
            pltpu.VMEM((planes + 2, views, G, pixels), f32),
            pltpu.VMEM((planes + 2, views, G, pixels), f32),
            pltpu.VMEM((planes, G, pixels), f32),
            pltpu.VMEM((3 * G, G, LANES), f32),
            pltpu.VMEM((3 * G, G, LANES), f32),
            pltpu.VMEM((planes, 2 * rows, pixels), bf16),
            pltpu.VMEM((2 * rows, pixels), f32),
            pltpu.VMEM((channels, pixels), f32),
            pltpu.VMEM((2, views, full, pixels), bf16),
            pltpu.VMEM((2, n_plane - 1, views, full, LANES), bf16),
            pltpu.VMEM((views, full, LANES), bf16),
            pltpu.VMEM((2 * views * full, LANES), f32),
            pltpu.VMEM((2 * chips * views * half, LANES), f32),
            pltpu.VMEM((chips, 2, views * half, LANES), bf16),
            pltpu.VMEM((chips, 2, views * half, LANES), bf16),
            pltpu.VMEM((2, views * half, LANES), f32),
            pltpu.VMEM((2, views * half, LANES), bf16),
            pltpu.VMEM((n_plane, 2, views * half, LANES), bf16),
            pltpu.VMEM((n_plane, views * channels, LANES), f32),
            pltpu.VMEM((2 * chips * views, 2 * LANES), bf16),
            dma, dma,
            dma((n_view,)), dma((n_view,)),
            dma((views, n_plane, 2)), dma((views, n_plane, 2)), dma((views,)), dma((views,)),
            dma((views, 2)), dma((views, 2)), dma((views, 2)), dma((views, 2)),
            dma((views, n_plane, 2)), dma((views, n_plane, 2)), dma((views,)), dma((views,)),
            dma((chips,)), dma((chips,)), dma((2, n_plane)), dma((n_plane, 2)),
        ],
        compiler_params=pltpu.CompilerParams(collective_id=0, has_side_effects=True),
        name="plane_sweep",
    )(features, sources.T, warp_weights, view_gate.reshape(1, G), depth_kernel, cotangent)


def solution(mesh):
    in_specs = (
        P("view", None, None),
        P(),
        P("plane", None, None),
        P(),
        P(),
        P("view", "plane", None, None),
    )
    out_specs = (P("view", "plane", None, None), P("view", None, None))
    body = functools.partial(shards, mesh.shape["view"], mesh.shape["plane"])
    return jax.shard_map(body, mesh=mesh, in_specs=in_specs, out_specs=out_specs, check_vma=False)
```
